32 devices in a mesh: wide: 8 (over z, y), narrow: 4 (over x, core).
Axes of the slice: x: 2, y: 2, z: 4, core: 2. Of those that a mesh axis runs over, the one named last changes fastest.
Arguments:
- mobility: float32 [128, 64, 256], P('wide', 'narrow'), may hold values from 0.2 to 5
- sav_vector: float32 [128, 64, 256], P('wide', 'narrow'), may hold values from -8 to 8
- cotangent: float32 [128, 64, 256], P('wide', 'narrow'), may hold values from -8 to 8
Outputs:
- adjoint: float32 [128, 64, 256], P('wide', 'narrow')
The draws below stay inside these ranges and needn't reach their ends.
All inputs are finite; a program needn't handle non-finite values.
Results may differ from the reference program's by a relative error of at most 0.0019.
Values sent between devices are 32-bit elements; how exact they have to be, the bound alone decides.
A program may use at most 128 MiB of HBM per device.

```python
import math
import jax
import jax.numpy as jnp

NZ = 256
LEVELS = 5
NX = 128
NY = 64


def shared_part(key):
    return jax.random.normal(jax.random.fold_in(key, 7), (NX, NY, NZ), jnp.float32)


def draw_sav_vector(key, part):
    own_part = jax.random.normal(jax.random.fold_in(key, 11), (NX, NY, NZ), jnp.float32)
    return jnp.clip(shared_part(key) + 0.7 * own_part, -8.0, 8.0)


def draw_cotangent(key, part):
    own_part = jax.random.normal(jax.random.fold_in(key, 13), (NX, NY, NZ), jnp.float32)
    return jnp.clip(shared_part(key) + 0.7 * own_part, -8.0, 8.0)


def level_of(rng, dims, split, least, high):
    gain = 1.0
    for dim, blocks in split:
        steps = jax.random.uniform(jax.random.fold_in(jax.random.fold_in(rng, 6), dim), (blocks,), jnp.float32, least / len(split), high / len(split))
        gain = gain * jnp.repeat(jnp.exp(steps), dims[dim] // blocks).reshape((-1,) + (1,) * (len(dims) - 1 - dim))
    return gain


def setup_inputs(seed: int = 0) -> dict:
    seeds = jax.random.split(jax.random.key(seed), 4)
    mobility = jnp.clip(jnp.exp(math.log(5.0) - 3.218876 * jax.random.uniform(seeds[0], (NX, NY, NZ), jnp.float32) ** level_of(seeds[0], (NX, NY, NZ), ((0, 8), (1, 4)), -0.2, 0.2)), 0.2, 5.0)
    sav_vector = draw_sav_vector(jax.random.fold_in(seeds[3], 71), 0)
    cotangent = draw_cotangent(jax.random.fold_in(seeds[3], 71), 0)
    return {"mobility": mobility, "sav_vector": sav_vector, "cotangent": cotangent}


DAMPING = 0.8
BASE_TAU = 16.0


def face_terms(padded, tau):
    center = padded[1:-1, 1:-1, 1:-1]
    others = [padded[2:, 1:-1, 1:-1], padded[:-2, 1:-1, 1:-1], padded[1:-1, 2:, 1:-1],
              padded[1:-1, :-2, 1:-1], padded[1:-1, 1:-1, 2:], padded[1:-1, 1:-1, :-2]]
    couplings = jnp.stack([(0.5 * tau) * (center + other) for other in others]).astype(jnp.bfloat16)
    diagonal = jnp.float32(1.0) + couplings[0].astype(jnp.float32)
    for index in range(1, 6):
        diagonal = diagonal + couplings[index].astype(jnp.float32)
    return couplings, diagonal


def coarsen(values):
    count, size_x, size_y, size_z = values.shape
    blocks = values.reshape(count, size_x // 2, 2, size_y // 2, 2, size_z // 2, 2)
    return blocks.mean(axis=(2, 4, 6))


def refine(values):
    return jnp.repeat(jnp.repeat(jnp.repeat(values, 2, axis=1), 2, axis=2), 2, axis=3)


def operate(iterate, couplings, diagonal):
    padded = jnp.pad(iterate, ((0, 0), (1, 1), (1, 1), (1, 1)))
    others = [padded[:, 2:, 1:-1, 1:-1], padded[:, :-2, 1:-1, 1:-1], padded[:, 1:-1, 2:, 1:-1],
              padded[:, 1:-1, :-2, 1:-1], padded[:, 1:-1, 1:-1, 2:], padded[:, 1:-1, 1:-1, :-2]]
    total = couplings[0].astype(jnp.float32)[None] * others[0]
    for index in range(1, 6):
        total = total + couplings[index].astype(jnp.float32)[None] * others[index]
    return diagonal[None] * iterate - total


def relax_once(iterate, source, couplings, diagonal):
    return iterate + DAMPING * (source - operate(iterate, couplings, diagonal)) / diagonal[None]


def multigrid(source, level_index, operators):
    couplings, diagonal = operators[level_index]
    iterate = DAMPING * source / diagonal[None]
    if level_index == LEVELS - 1:
        return relax_once(iterate, source, couplings, diagonal)
    iterate = relax_once(iterate, source, couplings, diagonal)
    residual = source - operate(iterate, couplings, diagonal)
    correction = multigrid(coarsen(residual), level_index + 1, operators)
    iterate = iterate + refine(correction)
    iterate = relax_once(iterate, source, couplings, diagonal)
    return relax_once(iterate, source, couplings, diagonal)


def reference(mobility, sav_vector, cotangent):
    operators = []
    mobile = mobility
    for level_index in range(LEVELS):
        operators.append(face_terms(jnp.pad(mobile, 1), BASE_TAU / 4.0 ** level_index))
        if level_index + 1 < LEVELS:
            mobile = coarsen(mobile[None])[0]
    adjoint_b = multigrid(sav_vector[None], 0, operators)[0]
    numerator = jnp.sum(adjoint_b * cotangent)
    denominator = jnp.sum(sav_vector * adjoint_b)
    sav_ratio = numerator / (1.0 + denominator)
    return multigrid((cotangent - sav_ratio * sav_vector)[None], 0, operators)[0]
```

```python
import functools
import jax
import jax.numpy as jnp
from jax import lax
from jax.experimental import pallas as pl
from jax.experimental.pallas import tpu as pltpu
from jax.sharding import PartitionSpec as P

DAMPING = 0.8
KEEP = 1.0 - DAMPING
BASE_TAU = 16.0
H0 = 4
H1 = 5
PAD = 2
MESH = pl.DeviceIdType.MESH
F32 = jnp.float32
SIDES = [(-1, 0), (1, 0), (0, -1), (0, 1), (-1, -1), (-1, 1), (1, -1), (1, 1)]
OPPOSITE = [1, 0, 3, 2, 7, 6, 5, 4]


def iota(shape, dim):
    return lax.broadcasted_iota(jnp.int32, shape, dim)


def shift(value, amount, axis):
    return pltpu.roll(value, amount % value.shape[axis], axis)


def squeeze_matrix(rows, cols, offset=0):
    i, j = iota((rows, cols), 0), iota((rows, cols), 1)
    k = i - 2 * (j - offset)
    return jnp.where((k == 0) | (k == 1), 1.0, 0.0).astype(F32)


def spread_matrix(rows, cols):
    i, j = iota((rows, cols), 0), iota((rows, cols), 1)
    k = j - 2 * i
    return jnp.where((k == 0) | (k == 1), 1.0, 0.0).astype(F32)


def mm(a, b):
    return jnp.dot(a, b, precision=lax.Precision.HIGHEST, preferred_element_type=F32)


def rounded(x):
    return x.astype(jnp.bfloat16).astype(F32)


def slabs(lo, hi, chunk, body):
    def step(i, _):
        for k in range(chunk):
            body(lo + i * chunk + k)
        return 0

    lax.fori_loop(0, (hi - lo) // chunk, step, 0)


def build(m, cx, cy, cz, rd, d, lo, hi, tau, seg, chunk):
    shape = m.shape[1:]
    row = iota(shape, 0)
    lane = lax.rem(iota(shape, 1), seg)
    last_row, first_row = row == shape[0] - 1, row == 0
    last_lane, first_lane = lane == seg - 1, lane == 0
    half = 0.5 * tau

    def body(a):
        own = m[a]
        xp, xm = m[a + 1], m[a - 1]
        yp = jnp.where(last_row, 0.0, shift(own, -1, 0))
        ym = jnp.where(first_row, 0.0, shift(own, 1, 0))
        zp = jnp.where(last_lane, 0.0, shift(own, -1, 1))
        zm = jnp.where(first_lane, 0.0, shift(own, 1, 1))
        total = 1.0
        for other, ref in ((xp, cx), (xm, None), (yp, cy), (ym, None), (zp, cz), (zm, None)):
            face = rounded(half * (own + other))
            total = total + face
            if ref is not None:
                ref[a] = jnp.where(jnp.minimum(own, other) > 0.0, face, 0.0)
        rd[a] = DAMPING / total
        if d is not None:
            d[a] = total

    slabs(lo, hi, chunk, body)


def neighbours(v, a, cx, cy, cz):
    own = v[a]
    cya, cza = cy[a], cz[a]
    total = cx[a] * v[a + 1] + cx[a - 1] * v[a - 1]
    total = total + (cya * shift(own, -1, 0) + shift(cya * own, 1, 0))
    total = total + (cza * shift(own, -1, 1) + shift(cza * own, 1, 1))
    return own, total


def sweep(vin, vout, r, ops, lo, hi, chunk):
    cx, cy, cz, rd, d = ops

    def body(a):
        for vi, vo, ri in zip(vin, vout, r):
            own, t = neighbours(vi, a, cx, cy, cz)
            vo[a] = KEEP * own + rd[a] * (ri[a] + t)

    slabs(lo, hi, chunk, body)


def residual(vi, ri, a, ops):
    cx, cy, cz, rd, d = ops
    own, t = neighbours(vi, a, cx, cy, cz)
    diag = d[a] if d is not None else DAMPING / rd[a]
    return own, ri[a] + t - diag * own


def fold(x):
    total = None
    for i in range(x.shape[0] // 8):
        for j in range(x.shape[1] // 128):
            part = x[8 * i : 8 * i + 8, 128 * j : 128 * j + 128]
            total = part if total is None else total + part
    return total


def kernel(nw, nn, bx, by, nz, m_ref, s_ref, c_ref, out_ref,
           m0, cx0, cy0, cz0, rd0, d0, rs0, rc0, us0, uc0, vs0, vc0,
           rx, yp, ry, cp, rcn,
           m1, cx1, cy1, cz1, rd1, d1, r1, u1, v1, w1,
           cx2, cy2, cz2, rd2, r2, u2, v2,
           cx3, cy3, cz3, rd3, r3, u3, v3,
           cx4, cy4, cz4, rd4, r4, u4, v4,
           t0, t0y, t1, t1y, sm2, sr2, sp2, gm, gr, gp, pb, pbs, t2, t2y, f1, f1p, f0a, f0b,
           e0s, e0r, m1s, m1r, e1s, e1r,
           ams, amr, bms, bmr, ars, arr, aps, apr, brs, brr, bps, bpr):
    iw, ino = lax.axis_index("wide"), lax.axis_index("narrow")
    b1x, b1y, z1 = bx // 2, by // 2, nz // 2
    b2x, b2y, z2 = bx // 4, by // 4, nz // 4
    x2, x3, x4 = nw * b2x, nw * b2x // 2, nw * b2x // 4
    xs0 = bx + 2 * H0
    there = []
    for dx, dy in SIDES:
        ok = None
        for cond, on in ((iw > 0, dx < 0), (iw < nw - 1, dx > 0), (ino > 0, dy < 0), (ino < nn - 1, dy > 0)):
            if on:
                ok = cond if ok is None else jnp.logical_and(ok, cond)
        there.append(ok)

    def peer(side):
        return (iw + SIDES[side][0], ino + SIDES[side][1])

    barrier = pltpu.get_barrier_semaphore()

    def greet(j, _):
        pl.semaphore_signal(barrier, inc=1, device_id=(lax.rem(iw + j, nw), ino), device_id_type=MESH)
        return 0

    lax.fori_loop(1, nw, greet, 0)
    for j in range(1, nn):
        pl.semaphore_signal(barrier, inc=1, device_id=(iw, lax.rem(ino + j, nn)), device_id_type=MESH)
    for k in range(4, 8):
        @pl.when(there[k])
        def _():
            pl.semaphore_signal(barrier, inc=1, device_id=peer(k), device_id_type=MESH)

    for side, (m_lo, r_lo) in enumerate(((0, 0), (by - 4, by - 3))):
        for k in range(4):
            yp[side, k] = m_ref[:, m_lo + k, :]
        for k in range(3):
            yp[side, 4 + k] = s_ref[:, r_lo + k, :]
            yp[side, 7 + k] = c_ref[:, r_lo + k, :]
    for k in range(4, 8):
        dx, dy = SIDES[k]
        m_x, m_y = (0 if dx < 0 else bx - 3), (0 if dy < 0 else by - 3)
        r_x, r_y = (0 if dx < 0 else bx - 2), (0 if dy < 0 else by - 2)
        for i in range(3):
            cp[k - 4, 3 * i : 3 * i + 3, :] = m_ref[m_x + i, m_y : m_y + 3, :]
        for i in range(2):
            cp[k - 4, 9 + 2 * i : 11 + 2 * i, :] = s_ref[r_x + i, r_y : r_y + 2, :]
            cp[k - 4, 13 + 2 * i : 15 + 2 * i, :] = c_ref[r_x + i, r_y : r_y + 2, :]

    beside_x = jnp.minimum(iw, 1) + jnp.minimum(nw - 1 - iw, 1)
    beside_y = jnp.minimum(ino, 1) + jnp.minimum(nn - 1 - ino, 1)
    pl.semaphore_wait(barrier, nw + nn - 2 + beside_x * beside_y)

    def remote(src, dst, ssem, rsem, dev):
        return pltpu.make_async_remote_copy(src_ref=src, dst_ref=dst, send_sem=ssem, recv_sem=rsem,
                                            device_id=dev, device_id_type=MESH)

    def e0_copies(side, recv):
        other = OPPOSITE[side]
        land = side if recv else other
        dev = peer(side)
        if side < 2:
            out = []
            at = 0
            for n, (ref, width) in enumerate(((m_ref, 4), (s_ref, 3), (c_ref, 3))):
                lo = 0 if side == 0 else bx - width
                out.append(remote(ref.at[lo : lo + width], rx.at[land, at : at + width],
                                  e0s.at[side, n], e0r.at[land, n], dev))
                at += width
            return out
        if side < 4:
            return [remote(yp.at[side - 2], ry.at[land - 2], e0s.at[side, 0], e0r.at[land, 0], dev)]
        return [remote(cp.at[side - 4], rcn.at[land - 4], e0s.at[side, 0], e0r.at[land, 0], dev)]

    def box1(side, sending, width):
        dx, dy = SIDES[side]
        own = H1
        if sending:
            xlo, w = (own, width) if dx < 0 else ((own + b1x - width, width) if dx > 0 else (own, b1x))
            ylo = b1y
        else:
            xlo, w = (own - width, width) if dx < 0 else ((own + b1x, width) if dx > 0 else (own, b1x))
            ylo = b1y * (1 + dy)
        return xlo, w, ylo

    def level1_copies(ref, ssem, rsem, side, recv, width):
        land = side if recv else OPPOSITE[side]
        sx, w, sy = box1(side, True, width)
        tx, _, ty = box1(land, False, width)
        return [remote(ref.at[v, sx : sx + w, sy : sy + b1y], ref.at[v, tx : tx + w, ty : ty + b1y],
                       ssem.at[side, v], rsem.at[land, v], peer(side)) for v in range(ref.shape[0])]

    def each(fn, act):
        for side in range(8):
            @pl.when(there[side])
            def _():
                for copy in fn(side):
                    act(copy)

    def start(copy):
        copy.start()

    each(lambda k: e0_copies(k, False), start)

    zc0 = squeeze_matrix(nz, z1)
    zc1 = squeeze_matrix(z1, z1)
    zc1b = squeeze_matrix(z1, z1, z2)
    zr = spread_matrix(z1, z1)

    def pair_rows(flat, half_rows):
        return flat[pl.ds(0, half_rows, stride=2), :] + flat[pl.ds(1, half_rows, stride=2), :]

    for i in range(b1x):
        t0[0, i * by : (i + 1) * by, :] = m_ref[2 * i] + m_ref[2 * i + 1]
    t0y[...] = mm(t0[0], zc0)
    mob1 = 0.125 * pair_rows(t0y, b1x * b1y)
    for i in range(b1x):
        m1[0, H1 + i, b1y : 2 * b1y, :] = mob1[i * b1y : (i + 1) * b1y]

    def clear1(ref, width):
        for side in range(8):
            xlo, w, ylo = box1(side, False, width)
            @pl.when(jnp.logical_not(there[side]))
            def _():
                ref[:, xlo : xlo + w, ylo : ylo + b1y, :] = jnp.zeros((ref.shape[0], w, b1y, z1), F32)

    clear1(m1, 5)
    clear1(r1, 4)
    each(lambda k: level1_copies(m1, m1s, m1r, k, False, 5), start)
    for i in range(b2x):
        t1[0, i * b1y : (i + 1) * b1y, :] = mob1[2 * i * b1y : (2 * i + 1) * b1y] + mob1[(2 * i + 1) * b1y : (2 * i + 2) * b1y]
    t1y[...] = mm(t1[0], zc1 + zc1b)
    mob2 = 0.125 * pair_rows(t1y, b2x * b2y)
    sm2[...] = mob2
    gm[ino, iw] = mob2

    def wide_copy(src, dst_ref, ssem, rsem, j, recv):
        to = lax.rem(iw + j, nw)
        if recv:
            return remote(src, dst_ref(to), ssem.at[j], rsem.at[to], (to, ino))
        return remote(src, dst_ref(iw), ssem.at[j], rsem.at[iw], (to, ino))

    def over_wide(src, dst_ref, ssem, rsem, what):
        def step(j, _):
            copy = wide_copy(src, dst_ref, ssem, rsem, j, what == "recv")
            if what == "start":
                copy.start()
            elif what == "recv":
                copy.wait_recv()
            else:
                copy.wait_send()
            return 0

        lax.fori_loop(1, nw, step, 0)

    def over_narrow(src, dst_ref, ssem, rsem, what):
        for j in range(1, nn):
            to = lax.rem(ino + j, nn)
            if what == "recv":
                remote(src, dst_ref(to), ssem.at[j], rsem.at[to], (iw, to)).wait_recv()
            else:
                copy = remote(src, dst_ref(ino), ssem.at[j], rsem.at[ino], (iw, to))
                if what == "start":
                    copy.start()
                else:
                    copy.wait_send()

    gather_m = (sm2, lambda w: gm.at[ino, w], ams, amr)
    spread_m = (gm.at[ino], lambda n: gm.at[n], bms, bmr)
    gather_r = (sr2, lambda w: gr.at[ino, w], ars, arr)
    gather_p = (sp2, lambda w: gp.at[w], aps, apr)
    spread_r = (gr.at[ino], lambda n: gr.at[n], brs, brr)
    spread_p = (pb, lambda n: pbs.at[n], bps, bpr)
    over_wide(*gather_m, "start")

    blank = jnp.zeros((H0, m0.shape[1], nz), F32)
    for ref, src in ((m0, m_ref), (rs0, s_ref), (rc0, c_ref)):
        ref[0:H0] = blank
        ref[H0 + bx :] = blank

        def put(i, _):
            ref[H0 + i, H0 : H0 + by, :] = src[i]
            return 0

        lax.fori_loop(0, bx, put, 0)
    for ref in (u2, v2, u3, v3, u4, v4):
        zero = jnp.zeros(ref.shape[1:], F32)
        for a in (0, 1, ref.shape[0] - 2, ref.shape[0] - 1):
            ref[a] = zero
    for ref in (cx2, cx3, cx4):
        ref[PAD - 1] = jnp.zeros(ref.shape[1:], F32)
    for k in range(2):
        @pl.when(jnp.logical_not(there[k]))
        def _():
            rx[k] = jnp.zeros(rx.shape[1:], F32)

        @pl.when(jnp.logical_not(there[2 + k]))
        def _():
            ry[k] = jnp.zeros(ry.shape[1:], F32)
    for k in range(4):
        @pl.when(jnp.logical_not(there[4 + k]))
        def _():
            rcn[k] = jnp.zeros(rcn.shape[1:], F32)

    each(lambda k: e0_copies(k, True), lambda c: c.wait_recv())
    for k, ref, at, width in ((0, m0, 0, 4), (0, rs0, 4, 3), (0, rc0, 7, 3)):
        for i in range(width):
            ref[H0 - width + i, H0 : H0 + by, :] = rx[0, at + i]
            ref[H0 + bx + i, H0 : H0 + by, :] = rx[1, at + i]
            ref[H0 : H0 + bx, H0 - width + i, :] = ry[0, at + i]
            ref[H0 : H0 + bx, H0 + by + i, :] = ry[1, at + i]
    for k in range(4):
        dx, dy = SIDES[4 + k]
        m_x, m_y = (H0 - 3 if dx < 0 else H0 + bx), (H0 - 3 if dy < 0 else H0 + by)
        r_x, r_y = (H0 - 2 if dx < 0 else H0 + bx), (H0 - 2 if dy < 0 else H0 + by)
        for i in range(3):
            m0[m_x + i, m_y : m_y + 3, :] = rcn[k, 3 * i : 3 * i + 3, :]
        for i in range(2):
            rs0[r_x + i, r_y : r_y + 2, :] = rcn[k, 9 + 2 * i : 11 + 2 * i, :]
            rc0[r_x + i, r_y : r_y + 2, :] = rcn[k, 13 + 2 * i : 15 + 2 * i, :]

    ops0 = (cx0, cy0, cz0, rd0, d0)
    build(m0, cx0, cy0, cz0, rd0, d0, 1, xs0 - 1, BASE_TAU, nz, 1)

    def first0(a):
        us0[a] = rd0[a] * rs0[a]
        uc0[a] = rd0[a] * rc0[a]

    slabs(1, xs0 - 1, 1, first0)
    sweep((us0, uc0), (vs0, vc0), (rs0, rc0), ops0, 2, xs0 - 2, 1)

    def down0(i, carry):
        num, den = carry
        sums = []
        for k in range(2):
            a = H0 + 2 * i + k
            vs, es = residual(vs0, rs0, a, ops0)
            vc, ec = residual(vc0, rc0, a, ops0)
            rs = rs0[a]
            num = num + fold((ec * vs + vc * rs)[H0 : H0 + by])
            den = den + fold((es * vs + vs * rs)[H0 : H0 + by])
            sums.append((es, ec))
        at = pl.ds(pl.multiple_of(i * by, by), by)
        t0[0, at, :] = (sums[0][0] + sums[1][0])[H0 : H0 + by]
        t0[1, at, :] = (sums[0][1] + sums[1][1])[H0 : H0 + by]
        return num, den

    zero8 = jnp.zeros((8, 128), F32)
    num0, den0 = lax.fori_loop(0, b1x, down0, (zero8, zero8))
    for v in range(2):
        t0y[...] = mm(t0[v], zc0)
        coarse = 0.125 * pair_rows(t0y, b1x * b1y)
        for i in range(b1x):
            r1[v, H1 + i, b1y : 2 * b1y, :] = coarse[i * b1y : (i + 1) * b1y]
    each(lambda k: level1_copies(r1, e1s, e1r, k, False, 4), start)

    each(lambda k: level1_copies(m1, m1s, m1r, k, True, 5), lambda c: c.wait_recv())
    ops1 = (cx1, cy1, cz1, rd1, d1)
    build(m1.at[0], cx1, cy1, cz1, rd1, d1, 1, b1x + 2 * H1 - 1, BASE_TAU / 4, z1, 2)
    over_wide(*gather_m, "recv")
    over_narrow(*spread_m, "start")

    each(lambda k: level1_copies(r1, e1s, e1r, k, True, 4), lambda c: c.wait_recv())
    rr1 = (r1.at[0], r1.at[1])
    uu1 = (u1.at[0], u1.at[1])
    vv1 = (v1.at[0], v1.at[1])

    def first1(a):
        for v in range(2):
            u1[v, a] = rd1[a] * r1[v, a]

    slabs(1, b1x + 2 * H1 - 1, 2, first1)
    sweep(uu1, vv1, rr1, ops1, 2, b1x + 2 * H1 - 2, 2)
    num1, den1 = zero8, zero8
    own_y = slice(b1y, 2 * b1y)
    for i in range(b2x):
        pair = []
        for k in range(2):
            a = H1 + 2 * i + k
            vs, es = residual(vv1[0], rr1[0], a, ops1)
            vc, ec = residual(vv1[1], rr1[1], a, ops1)
            rs = r1[0, a]
            num1 = num1 + fold((ec * vs + vc * rs)[own_y])
            den1 = den1 + fold((es * vs + vs * rs)[own_y])
            pair.append((es, ec))
        for v in range(2):
            t1[v, i * b1y : (i + 1) * b1y, :] = (pair[0][v] + pair[1][v])[own_y]
    t1y[...] = mm(t1[0], zc1) + mm(t1[1], zc1b)
    own2 = 0.125 * pair_rows(t1y, b2x * b2y)
    sr2[...] = own2
    gr[ino, iw] = own2
    num_row = jnp.sum(num0 + 8.0 * num1, axis=0, keepdims=True)
    den_row = jnp.sum(den0 + 8.0 * den1, axis=0, keepdims=True)
    row8 = iota((8, 128), 0)
    part = jnp.where(row8 == 0, num_row, jnp.where(row8 == 1, den_row, 0.0))
    sp2[...] = part
    gp[iw] = part
    over_wide(*gather_r, "start")
    over_wide(*gather_p, "start")

    over_narrow(*spread_m, "recv")

    def unpack(src, dst):
        def step(w, _):
            for n in range(nn):
                for i in range(b2x):
                    dst[PAD + w * b2x + i, n * b2y : (n + 1) * b2y, :] = src[n, w, i * b2y : (i + 1) * b2y, :]
            return 0

        lax.fori_loop(0, nw, step, 0)

    unpack(gm, v2)
    build(v2, cx2, cy2, cz2, rd2, None, PAD, PAD + x2, BASE_TAU / 16, z2, 4)

    def coarsen_pairs(get, xc, rows, dst):
        half = rows // 2

        def step(g, _):
            for k in range(4):
                a = PAD + 2 * (4 * g + k)
                t2[k * rows : (k + 1) * rows, :] = get(a) + get(a + 1)
            t2y[0 : 4 * rows, :] = mm(t2[0 : 4 * rows, :], zc1)
            flat = 0.125 * (t2y[pl.ds(0, 4 * half, stride=2), :] + t2y[pl.ds(1, 4 * half, stride=2), :])
            for k in range(4):
                dst[PAD + 4 * g + k, 0:half, :] = flat[k * half : (k + 1) * half]
            return 0

        lax.fori_loop(0, xc // 4, step, 0)

    v4[...] = jnp.zeros(v4.shape, F32)
    r4[...] = jnp.zeros(r4.shape, F32)
    coarsen_pairs(lambda a: v2[a], x3, v2.shape[1], v3)
    build(v3, cx3, cy3, cz3, rd3, None, PAD, PAD + x3, BASE_TAU / 64, z2 // 2, 4)
    coarsen_pairs(lambda a: v3[a], x4, v3.shape[1], v4)
    build(v4, cx4, cy4, cz4, rd4, None, PAD, PAD + x4, BASE_TAU / 256, z2 // 4, 4)

    over_wide(*gather_r, "recv")
    over_narrow(*spread_r, "start")
    over_wide(*gather_p, "recv")
    total = gp[0]
    if nw <= 16:
        for w in range(1, nw):
            total = total + gp[w]
    else:
        total = lax.fori_loop(1, nw, lambda w, acc: acc + gp[w], total)
    pb[...] = total
    over_narrow(*spread_p, "start")
    over_narrow(*spread_r, "recv")
    unpack(gr, r2)

    ops2 = (cx2, cy2, cz2, rd2, None)
    ops3 = (cx3, cy3, cz3, rd3, None)
    ops4 = (cx4, cy4, cz4, rd4, None)

    def down(u, v, r, ops, xc):
        def first(a):
            u[a] = ops[3][a] * r[a]

        slabs(PAD, PAD + xc, 4, first)
        sweep((u,), (v,), (r,), ops, PAD, PAD + xc, 4)

    def up(v, coarse, xc, rows):
        half = rows // 2

        def step(g, _):
            for k in range(4):
                t2[8 * k : 8 * k + 8, :] = coarse[PAD + 4 * g + k]
            wide_rows = mm(t2[0:32, :], zr)
            t2y[pl.ds(0, 32, stride=2), :] = wide_rows
            t2y[pl.ds(1, 32, stride=2), :] = wide_rows
            for k in range(4):
                add = t2y[16 * k : 16 * k + rows, :]
                a = PAD + 2 * (4 * g + k)
                v[a] = v[a] + add
                v[a + 1] = v[a + 1] + add
            return 0

        lax.fori_loop(0, xc // 4, step, 0)

    down(u2, v2, r2, ops2, x2)
    coarsen_pairs(lambda a: residual(v2, r2, a, ops2)[1], x3, v2.shape[1], r3)
    down(u3, v3, r3, ops3, x3)
    coarsen_pairs(lambda a: residual(v3, r3, a, ops3)[1], x4, v3.shape[1], r4)
    down(u4, v4, r4, ops4, x4)
    up(v3, v4, x4, v3.shape[1])
    sweep((v3,), (u3,), (r3,), ops3, PAD, PAD + x3, 4)
    sweep((u3,), (v3,), (r3,), ops3, PAD, PAD + x3, 4)
    up(v2, v3, x3, v2.shape[1])
    sweep((v2,), (u2,), (r2,), ops2, PAD, PAD + x2, 4)
    sweep((u2,), (v2,), (r2,), ops2, PAD, PAD + x2, 4)

    low = iota(v2.shape[1:], 1) < z2

    def dots(i, carry):
        num, den = carry
        for k in range(4):
            a = PAD + 4 * i + k
            both = jnp.where(low, v2[a], 0.0)
            den = den + fold(both * r2[a])
            num = num + fold(both * shift(r2[a], z2, 1))
        return num, den

    num2, den2 = lax.fori_loop(0, x2 // 4, dots, (zero8, zero8))
    over_narrow(*spread_p, "recv")
    whole = total
    for j in range(1, nn):
        whole = whole + pbs[lax.rem(ino + j, nn)]
    num = jnp.sum(jnp.where(row8 == 0, whole, 0.0) + 64.0 * num2)
    den = jnp.sum(jnp.where(row8 == 1, whole, 0.0) + 64.0 * den2)
    ratio = (jnp.full((8, 128), num) / (1.0 + jnp.full((8, 128), den)))[0:1, :]

    rows2 = v2.shape[1]
    full_y = 2 * rows2
    for i in range(b2x + 4):
        e = v2[PAD + iw * b2x - 2 + i]
        f1[i * rows2 : (i + 1) * rows2, :] = shift(e, z2, 1) - ratio * e
    fine = mm(f1[...], zr)
    for i in range(b2x + 4):
        part = fine[i * rows2 : (i + 1) * rows2]
        f1p[i, 0:b1y, :] = jnp.zeros((b1y, z1), F32)
        f1p[i, b1y + full_y : 2 * b1y + full_y, :] = jnp.zeros((b1y, z1), F32)
        f1p[i, pl.ds(b1y, rows2, stride=2), :] = part
        f1p[i, pl.ds(b1y + 1, rows2, stride=2), :] = part
    window = pl.ds(pl.multiple_of(ino * b1y, 8), 3 * b1y)
    for a in range(2, b1x + 2 * H1 - 2):
        i = (a - H1) // 2 + 2
        u1[0, a] = v1[1, a] - ratio * v1[0, a] + f1p[i, window, :]
        w1[a] = r1[1, a] - ratio * r1[0, a]
    sweep((u1.at[0],), (u1.at[1],), (w1,), ops1, 3, b1x + 2 * H1 - 3, 2)
    sweep((u1.at[1],), (u1.at[0],), (w1,), ops1, 4, b1x + 2 * H1 - 4, 2)

    rows1 = 3 * b1y
    zr0 = spread_matrix(z1, nz)
    ratio0 = jnp.concatenate([ratio] * (nz // 128), axis=1)
    for i in range(b1x + 2):
        part = mm(u1[0, H1 - 1 + i], zr0)
        for ref, lanes in ((f0a, slice(0, 128)), (f0b, slice(128, 256))):
            ref[i, pl.ds(0, rows1, stride=2), :] = part[:, lanes]
            ref[i, pl.ds(1, rows1, stride=2), :] = part[:, lanes]
    y_at = 2 * b1y - H0

    def up0(i, _):
        add = jnp.concatenate([f0a[i, y_at : y_at + m0.shape[1], :], f0b[i, y_at : y_at + m0.shape[1], :]], axis=1)
        for k in range(2):
            a = H0 - 2 + 2 * i + k
            us0[a] = vc0[a] - ratio0 * vs0[a] + add
            rc0[a] = rc0[a] - ratio0 * rs0[a]
        return 0

    lax.fori_loop(0, b1x + 2, up0, 0)
    sweep((us0,), (uc0,), (rc0,), ops0, 3, xs0 - 3, 1)

    def last(a):
        own, t = neighbours(uc0, a, cx0, cy0, cz0)
        out_ref[a - H0] = (KEEP * own + rd0[a] * (rc0[a] + t))[H0 : H0 + by]

    slabs(H0, H0 + bx, 1, last)

    each(lambda k: e0_copies(k, False), lambda c: c.wait_send())
    each(lambda k: level1_copies(m1, m1s, m1r, k, False, 5), lambda c: c.wait_send())
    each(lambda k: level1_copies(r1, e1s, e1r, k, False, 4), lambda c: c.wait_send())
    over_wide(*gather_m, "send")
    over_wide(*gather_r, "send")
    over_wide(*gather_p, "send")
    over_narrow(*spread_m, "send")
    over_narrow(*spread_r, "send")
    over_narrow(*spread_p, "send")


def solution(mesh):
    nw, nn = mesh.shape["wide"], mesh.shape["narrow"]

    def per_device(mobility, sav_vector, cotangent):
        bx, by, nz = mobility.shape
        b1x, b1y, z1 = bx // 2, by // 2, nz // 2
        x2, y2 = nw * bx // 4, nn * by // 4
        vm = lambda *s: pltpu.VMEM(s, F32)
        dma = lambda *s: pltpu.SemaphoreType.DMA(s)
        l0 = (bx + 2 * H0, by + 2 * H0, nz)
        l1 = (b1x + 2 * H1, 3 * b1y, z1)
        l2 = (x2 + 2 * PAD, y2, z1)
        l3 = (x2 // 2 + 2 * PAD, y2 // 2, z1)
        l4 = (x2 // 4 + 2 * PAD, 8, z1)
        own2 = (bx // 4 * (by // 4), z1)
        scratch = (
            [vm(*l0)] * 12
            + [vm(2, 10, bx, nz), vm(2, 10, bx, nz), vm(2, 10, bx, nz), vm(4, 24, nz), vm(4, 24, nz)]
            + [vm(1, *l1)] + [vm(*l1)] * 5 + [vm(2, *l1)] * 3 + [vm(*l1)]
            + [vm(*l2)] * 7 + [vm(*l3)] * 7 + [vm(*l4)] * 7
            + [vm(2, b1x * by, nz), vm(b1x * by, z1), vm(2, bx // 4 * b1y, z1), vm(bx // 4 * b1y, z1)]
            + [vm(*own2), vm(*own2), vm(8, 128), vm(nn, nw, *own2), vm(nn, nw, *own2), vm(nw, 8, 128),
               vm(8, 128), vm(nn, 8, 128)]
            + [vm(64, z1), vm(64, z1)]
            + [vm((bx // 4 + 4) * y2, z1), vm(bx // 4 + 4, 2 * y2 + 2 * b1y, z1)]
            + [vm(b1x + 2, 6 * b1y, 128)] * 2
            + [dma(8, 3), dma(8, 3), dma(8, 1), dma(8, 1), dma(8, 2), dma(8, 2)]
            + [dma(nw), dma(nw), dma(nn), dma(nn)] + [dma(nw)] * 4 + [dma(nn)] * 4
        )
        return pl.pallas_call(
            functools.partial(kernel, nw, nn, bx, by, nz),
            out_shape=jax.ShapeDtypeStruct((bx, by, nz), F32),
            in_specs=[pl.BlockSpec(memory_space=pltpu.VMEM)] * 3,
            out_specs=pl.BlockSpec(memory_space=pltpu.VMEM),
            scratch_shapes=scratch,
            compiler_params=pltpu.CompilerParams(
                collective_id=0, has_side_effects=True, vmem_limit_bytes=67043328
            ),
        )(mobility, sav_vector, cotangent)

    spec = P("wide", "narrow", None)
    return jax.shard_map(per_device, mesh=mesh, in_specs=(spec,) * 3, out_specs=spec, check_vma=False)
```

```python
import functools
import jax
import jax.numpy as jnp
from jax import lax
from jax.experimental import pallas as pl
from jax.experimental.pallas import tpu as pltpu
from jax.sharding import PartitionSpec as P

DAMPING = 0.8
KEEP = 1.0 - DAMPING
BASE_TAU = 16.0
H0 = 4
H1 = 5
PAD = 2
MESH = pl.DeviceIdType.MESH
F32 = jnp.float32
SIDES = [(-1, 0), (1, 0), (0, -1), (0, 1), (-1, -1), (-1, 1), (1, -1), (1, 1)]
OPPOSITE = [1, 0, 3, 2, 7, 6, 5, 4]


def iota(shape, dim):
    return lax.broadcasted_iota(jnp.int32, shape, dim)


def shift(value, amount, axis):
    return pltpu.roll(value, amount % value.shape[axis], axis)


def squeeze_matrix(rows, cols, offset=0):
    i, j = iota((rows, cols), 0), iota((rows, cols), 1)
    k = i - 2 * (j - offset)
    return jnp.where((k == 0) | (k == 1), 1.0, 0.0).astype(F32)


def spread_matrix(rows, cols):
    i, j = iota((rows, cols), 0), iota((rows, cols), 1)
    k = j - 2 * i
    return jnp.where((k == 0) | (k == 1), 1.0, 0.0).astype(F32)


def mm(a, b):
    return jnp.dot(a, b, precision=lax.Precision.HIGHEST, preferred_element_type=F32)


def rounded(x):
    return x.astype(jnp.bfloat16).astype(F32)


def slabs(lo, hi, chunk, body):
    def step(i, _):
        for k in range(chunk):
            body(lo + i * chunk + k)
        return 0

    lax.fori_loop(0, (hi - lo) // chunk, step, 0)


def build(m, cx, cy, cz, rd, d, lo, hi, tau, seg, chunk):
    shape = m.shape[1:]
    row = iota(shape, 0)
    lane = lax.rem(iota(shape, 1), seg)
    last_row, first_row = row == shape[0] - 1, row == 0
    last_lane, first_lane = lane == seg - 1, lane == 0
    half = 0.5 * tau

    def body(a):
        own = m[a]
        xp, xm = m[a + 1], m[a - 1]
        yp = jnp.where(last_row, 0.0, shift(own, -1, 0))
        ym = jnp.where(first_row, 0.0, shift(own, 1, 0))
        zp = jnp.where(last_lane, 0.0, shift(own, -1, 1))
        zm = jnp.where(first_lane, 0.0, shift(own, 1, 1))
        total = 1.0
        for other, ref in ((xp, cx), (xm, None), (yp, cy), (ym, None), (zp, cz), (zm, None)):
            face = rounded(half * (own + other))
            total = total + face
            if ref is not None:
                ref[a] = jnp.where(jnp.minimum(own, other) > 0.0, face, 0.0)
        rd[a] = DAMPING / total
        if d is not None:
            d[a] = total

    slabs(lo, hi, chunk, body)


def neighbours(v, a, cx, cy, cz):
    own = v[a]
    cya, cza = cy[a], cz[a]
    total = cx[a] * v[a + 1] + cx[a - 1] * v[a - 1]
    total = total + (cya * shift(own, -1, 0) + shift(cya * own, 1, 0))
    total = total + (cza * shift(own, -1, 1) + shift(cza * own, 1, 1))
    return own, total


def sweep(vin, vout, r, ops, lo, hi, chunk):
    cx, cy, cz, rd, d = ops

    def body(a):
        for vi, vo, ri in zip(vin, vout, r):
            own, t = neighbours(vi, a, cx, cy, cz)
            vo[a] = KEEP * own + rd[a] * (ri[a] + t)

    slabs(lo, hi, chunk, body)


def residual(vi, ri, a, ops):
    cx, cy, cz, rd, d = ops
    own, t = neighbours(vi, a, cx, cy, cz)
    diag = d[a] if d is not None else DAMPING / rd[a]
    return own, ri[a] + t - diag * own


def fold(x):
    total = None
    for i in range(x.shape[0] // 8):
        for j in range(x.shape[1] // 128):
            part = x[8 * i : 8 * i + 8, 128 * j : 128 * j + 128]
            total = part if total is None else total + part
    return total


def kernel(nw, nn, bx, by, nz, m_ref, s_ref, c_ref, out_ref,
           m0, cx0, cy0, cz0, rd0, d0, rs0, rc0, us0, uc0, vs0, vc0,
           rx, yp, ry, cp, rcn,
           m1, cx1, cy1, cz1, rd1, d1, r1, u1, v1, w1,
           cx2, cy2, cz2, rd2, r2, u2, v2,
           cx3, cy3, cz3, rd3, r3, u3, v3,
           cx4, cy4, cz4, rd4, r4, u4, v4,
           t0, t0y, t1, t1y, sm2, sr2, sp2, gm, gr, gp, pb, pbs, t2, t2y, f1, f1p, f0a, f0b,
           e0s, e0r, m1s, m1r, e1s, e1r,
           ams, amr, bms, bmr, ars, arr, aps, apr, brs, brr, bps, bpr):
    iw, ino = lax.axis_index("wide"), lax.axis_index("narrow")
    b1x, b1y, z1 = bx // 2, by // 2, nz // 2
    b2x, b2y, z2 = bx // 4, by // 4, nz // 4
    x2, x3, x4 = nw * b2x, nw * b2x // 2, nw * b2x // 4
    xs0 = bx + 2 * H0
    there = []
    for dx, dy in SIDES:
        ok = None
        for cond, on in ((iw > 0, dx < 0), (iw < nw - 1, dx > 0), (ino > 0, dy < 0), (ino < nn - 1, dy > 0)):
            if on:
                ok = cond if ok is None else jnp.logical_and(ok, cond)
        there.append(ok)

    def peer(side):
        return (iw + SIDES[side][0], ino + SIDES[side][1])

    barrier = pltpu.get_barrier_semaphore()

    def greet(j, _):
        pl.semaphore_signal(barrier, inc=1, device_id=(lax.rem(iw + j, nw), ino), device_id_type=MESH)
        return 0

    lax.fori_loop(1, nw, greet, 0)
    for j in range(1, nn):
        pl.semaphore_signal(barrier, inc=1, device_id=(iw, lax.rem(ino + j, nn)), device_id_type=MESH)
    for k in range(4, 8):
        @pl.when(there[k])
        def _():
            pl.semaphore_signal(barrier, inc=1, device_id=peer(k), device_id_type=MESH)

    for side, (m_lo, r_lo) in enumerate(((0, 0), (by - 4, by - 3))):
        for k in range(4):
            yp[side, k] = m_ref[:, m_lo + k, :]
        for k in range(3):
            yp[side, 4 + k] = s_ref[:, r_lo + k, :]
            yp[side, 7 + k] = c_ref[:, r_lo + k, :]
    for k in range(4, 8):
        dx, dy = SIDES[k]
        m_x, m_y = (0 if dx < 0 else bx - 3), (0 if dy < 0 else by - 3)
        r_x, r_y = (0 if dx < 0 else bx - 2), (0 if dy < 0 else by - 2)
        for i in range(3):
            cp[k - 4, 3 * i : 3 * i + 3, :] = m_ref[m_x + i, m_y : m_y + 3, :]
        for i in range(2):
            cp[k - 4, 9 + 2 * i : 11 + 2 * i, :] = s_ref[r_x + i, r_y : r_y + 2, :]
            cp[k - 4, 13 + 2 * i : 15 + 2 * i, :] = c_ref[r_x + i, r_y : r_y + 2, :]

    beside_x = jnp.minimum(iw, 1) + jnp.minimum(nw - 1 - iw, 1)
    beside_y = jnp.minimum(ino, 1) + jnp.minimum(nn - 1 - ino, 1)
    pl.semaphore_wait(barrier, nw + nn - 2 + beside_x * beside_y)

    def remote(src, dst, ssem, rsem, dev):
        return pltpu.make_async_remote_copy(src_ref=src, dst_ref=dst, send_sem=ssem, recv_sem=rsem,
                                            device_id=dev, device_id_type=MESH)

    def e0_copies(side, recv, wave=0):
        other = OPPOSITE[side]
        land = side if recv else other
        dev = peer(side)
        if side < 2:
            out = []
            at = 0
            for n, (ref, width) in enumerate(((m_ref, 4), (s_ref, 3), (c_ref, 3))):
                lo = 0 if side == 0 else bx - width
                skip = width - 1 if side == 0 else 0
                first = 0 if side == 0 else 1
                if wave == 1:
                    out.append(remote(ref.at[lo + skip : lo + skip + 1], rx.at[land, at + skip : at + skip + 1],
                                      e0s.at[side, 3 + n], e0r.at[land, 3 + n], dev))
                else:
                    out.append(remote(ref.at[lo + first : lo + first + width - 1],
                                      rx.at[land, at + first : at + first + width - 1],
                                      e0s.at[side, n], e0r.at[land, n], dev))
                at += width
            return out
        if side < 4:
            return [remote(yp.at[side - 2], ry.at[land - 2], e0s.at[side, 0], e0r.at[land, 0], dev)]
        return [remote(cp.at[side - 4], rcn.at[land - 4], e0s.at[side, 0], e0r.at[land, 0], dev)]

    def box1(side, sending, width):
        dx, dy = SIDES[side]
        own = H1
        if sending:
            xlo, w = (own, width) if dx < 0 else ((own + b1x - width, width) if dx > 0 else (own, b1x))
            ylo = b1y
        else:
            xlo, w = (own - width, width) if dx < 0 else ((own + b1x, width) if dx > 0 else (own, b1x))
            ylo = b1y * (1 + dy)
        return xlo, w, ylo

    def level1_copies(ref, ssem, rsem, side, recv, width):
        land = side if recv else OPPOSITE[side]
        sx, w, sy = box1(side, True, width)
        tx, _, ty = box1(land, False, width)
        return [remote(ref.at[v, sx : sx + w, sy : sy + b1y], ref.at[v, tx : tx + w, ty : ty + b1y],
                       ssem.at[side, v], rsem.at[land, v], peer(side)) for v in range(ref.shape[0])]

    def each(fn, act, sides=range(8)):
        for side in sides:
            @pl.when(there[side])
            def _():
                for copy in fn(side):
                    act(copy)

    def start(copy):
        copy.start()

    each(lambda k: e0_copies(k, False), start, (0, 1, 4, 5, 6, 7, 2, 3))

    zc0 = squeeze_matrix(nz, z1)
    zc1 = squeeze_matrix(z1, z1)
    zc1b = squeeze_matrix(z1, z1, z2)
    zr = spread_matrix(z1, z1)

    def pair_rows(flat, half_rows):
        return flat[pl.ds(0, half_rows, stride=2), :] + flat[pl.ds(1, half_rows, stride=2), :]

    for i in range(b1x):
        t0[0, i * by : (i + 1) * by, :] = m_ref[2 * i] + m_ref[2 * i + 1]
    t0y[...] = mm(t0[0], zc0)
    mob1 = 0.125 * pair_rows(t0y, b1x * b1y)
    for i in range(b1x):
        m1[0, H1 + i, b1y : 2 * b1y, :] = mob1[i * b1y : (i + 1) * b1y]

    def clear1(ref, width):
        for side in range(8):
            xlo, w, ylo = box1(side, False, width)
            @pl.when(jnp.logical_not(there[side]))
            def _():
                ref[:, xlo : xlo + w, ylo : ylo + b1y, :] = jnp.zeros((ref.shape[0], w, b1y, z1), F32)

    clear1(m1, 5)
    clear1(r1, 4)
    each(lambda k: level1_copies(m1, m1s, m1r, k, False, 5), start)
    for i in range(b2x):
        t1[0, i * b1y : (i + 1) * b1y, :] = mob1[2 * i * b1y : (2 * i + 1) * b1y] + mob1[(2 * i + 1) * b1y : (2 * i + 2) * b1y]
    t1y[...] = mm(t1[0], zc1 + zc1b)
    mob2 = 0.125 * pair_rows(t1y, b2x * b2y)
    sm2[...] = mob2
    gm[ino, iw] = mob2

    def wide_copy(src, dst_ref, ssem, rsem, j, recv):
        to = lax.rem(iw + j, nw)
        if recv:
            return remote(src, dst_ref(to), ssem.at[j], rsem.at[to], (to, ino))
        return remote(src, dst_ref(iw), ssem.at[j], rsem.at[iw], (to, ino))

    def over_wide(src, dst_ref, ssem, rsem, what):
        def step(j, _):
            copy = wide_copy(src, dst_ref, ssem, rsem, j, what == "recv")
            if what == "start":
                copy.start()
            elif what == "recv":
                copy.wait_recv()
            else:
                copy.wait_send()
            return 0

        lax.fori_loop(1, nw, step, 0)

    def over_narrow(src, dst_ref, ssem, rsem, what):
        for j in range(1, nn):
            to = lax.rem(ino + j, nn)
            if what == "recv":
                remote(src, dst_ref(to), ssem.at[j], rsem.at[to], (iw, to)).wait_recv()
            else:
                copy = remote(src, dst_ref(ino), ssem.at[j], rsem.at[ino], (iw, to))
                if what == "start":
                    copy.start()
                else:
                    copy.wait_send()

    gather_m = (sm2, lambda w: gm.at[ino, w], ams, amr)
    spread_m = (gm.at[ino], lambda n: gm.at[n], bms, bmr)
    gather_r = (sr2, lambda w: gr.at[ino, w], ars, arr)
    gather_p = (sp2, lambda w: gp.at[w], aps, apr)
    spread_r = (gr.at[ino], lambda n: gr.at[n], brs, brr)
    spread_p = (pb, lambda n: pbs.at[n], bps, bpr)
    each(lambda k: e0_copies(k, False, 1), start, (0, 1))
    over_wide(*gather_m, "start")

    blank = jnp.zeros((H0, m0.shape[1], nz), F32)
    for ref, src in ((m0, m_ref), (rs0, s_ref), (rc0, c_ref)):
        ref[0:H0] = blank
        ref[H0 + bx :] = blank

        def put(i, _):
            ref[H0 + i, H0 : H0 + by, :] = src[i]
            return 0

        lax.fori_loop(0, bx, put, 0)
    for ref in (u2, v2, u3, v3, u4, v4):
        zero = jnp.zeros(ref.shape[1:], F32)
        for a in (0, 1, ref.shape[0] - 2, ref.shape[0] - 1):
            ref[a] = zero
    for ref in (cx2, cx3, cx4):
        ref[PAD - 1] = jnp.zeros(ref.shape[1:], F32)
    for k in range(2):
        @pl.when(jnp.logical_not(there[k]))
        def _():
            rx[k] = jnp.zeros(rx.shape[1:], F32)

        @pl.when(jnp.logical_not(there[2 + k]))
        def _():
            ry[k] = jnp.zeros(ry.shape[1:], F32)
    for k in range(4):
        @pl.when(jnp.logical_not(there[4 + k]))
        def _():
            rcn[k] = jnp.zeros(rcn.shape[1:], F32)

    def landed(copy):
        copy.wait_recv()

    each(lambda k: e0_copies(k, True), landed, (2, 3))
    fields = ((m0, 0, 4), (rs0, 4, 3), (rc0, 7, 3))
    for ref, at, width in fields:
        for i in range(width):
            ref[H0 : H0 + bx, H0 - width + i, :] = ry[0, at + i]
            ref[H0 : H0 + bx, H0 + by + i, :] = ry[1, at + i]

    ops0 = (cx0, cy0, cz0, rd0, d0)

    def first0(a):
        us0[a] = rd0[a] * rs0[a]
        uc0[a] = rd0[a] * rc0[a]

    def start0(lo, hi, v_lo, v_hi):
        build(m0, cx0, cy0, cz0, rd0, d0, lo, hi, BASE_TAU, nz, 1)
        slabs(lo, hi, 1, first0)
        if v_hi > v_lo:
            sweep((us0, uc0), (vs0, vc0), (rs0, rc0), ops0, v_lo, v_hi, 1)

    start0(H0 + 1, H0 + bx - 1, H0 + 2, H0 + bx - 2)

    def down0(i, carry):
        num, den = carry
        sums = []
        for k in range(2):
            a = H0 + 2 * i + k
            vs, es = residual(vs0, rs0, a, ops0)
            vc, ec = residual(vc0, rc0, a, ops0)
            rs = rs0[a]
            num = num + fold((ec * vs + vc * rs)[H0 : H0 + by])
            den = den + fold((es * vs + vs * rs)[H0 : H0 + by])
            sums.append((es, ec))
        at = pl.ds(pl.multiple_of(i * by, by), by)
        t0[0, at, :] = (sums[0][0] + sums[1][0])[H0 : H0 + by]
        t0[1, at, :] = (sums[0][1] + sums[1][1])[H0 : H0 + by]
        return num, den

    zero8 = jnp.zeros((8, 128), F32)
    part0 = lax.fori_loop(2, b1x - 2, down0, (zero8, zero8))

    each(lambda k: e0_copies(k, True), landed, (0, 1, 4, 5, 6, 7))
    for ref, at, width in fields:
        for i in range(width - 1):
            ref[H0 - width + 1 + i, H0 : H0 + by, :] = rx[0, at + 1 + i]
            ref[H0 + bx + i, H0 : H0 + by, :] = rx[1, at + i]
    for k in range(4):
        dx, dy = SIDES[4 + k]
        m_x, m_y = (H0 - 3 if dx < 0 else H0 + bx), (H0 - 3 if dy < 0 else H0 + by)
        r_x, r_y = (H0 - 2 if dx < 0 else H0 + bx), (H0 - 2 if dy < 0 else H0 + by)
        for i in range(3):
            m0[m_x + i, m_y : m_y + 3, :] = rcn[k, 3 * i : 3 * i + 3, :]
        for i in range(2):
            rs0[r_x + i, r_y : r_y + 2, :] = rcn[k, 9 + 2 * i : 11 + 2 * i, :]
            rc0[r_x + i, r_y : r_y + 2, :] = rcn[k, 13 + 2 * i : 15 + 2 * i, :]
    for lo, hi, v_lo, v_hi in ((2, H0 + 1, 3, H0 + 2), (H0 + bx - 1, xs0 - 2, H0 + bx - 2, xs0 - 3)):
        build(m0, cx0, cy0, cz0, rd0, d0, lo, hi, BASE_TAU, nz, 1)
        slabs(lo, hi, 1, first0)
        sweep((us0, uc0), (vs0, vc0), (rs0, rc0), ops0, v_lo, v_hi, 1)
    part0 = lax.fori_loop(0, 2, down0, part0)
    num0, den0 = lax.fori_loop(b1x - 2, b1x, down0, part0)
    for v in range(2):
        t0y[...] = mm(t0[v], zc0)
        coarse = 0.125 * pair_rows(t0y, b1x * b1y)
        for i in range(b1x):
            r1[v, H1 + i, b1y : 2 * b1y, :] = coarse[i * b1y : (i + 1) * b1y]
    each(lambda k: level1_copies(r1, e1s, e1r, k, False, 4), start)

    each(lambda k: e0_copies(k, True, 1), landed, (0, 1))
    for ref, at, width in fields:
        ref[H0 - width, H0 : H0 + by, :] = rx[0, at]
        ref[H0 + bx + width - 1, H0 : H0 + by, :] = rx[1, at + width - 1]
    for lo, v_lo in ((1, 2), (xs0 - 2, xs0 - 3)):
        start0(lo, lo + 1, v_lo, v_lo + 1)
    each(lambda k: level1_copies(m1, m1s, m1r, k, True, 5), lambda c: c.wait_recv())
    ops1 = (cx1, cy1, cz1, rd1, d1)
    build(m1.at[0], cx1, cy1, cz1, rd1, d1, 1, b1x + 2 * H1 - 1, BASE_TAU / 4, z1, 2)
    over_wide(*gather_m, "recv")
    over_narrow(*spread_m, "start")

    each(lambda k: level1_copies(r1, e1s, e1r, k, True, 4), lambda c: c.wait_recv())
    rr1 = (r1.at[0], r1.at[1])
    uu1 = (u1.at[0], u1.at[1])
    vv1 = (v1.at[0], v1.at[1])

    def first1(a):
        for v in range(2):
            u1[v, a] = rd1[a] * r1[v, a]

    slabs(1, b1x + 2 * H1 - 1, 2, first1)
    sweep(uu1, vv1, rr1, ops1, 2, b1x + 2 * H1 - 2, 2)
    num1, den1 = zero8, zero8
    own_y = slice(b1y, 2 * b1y)
    for i in range(b2x):
        pair = []
        for k in range(2):
            a = H1 + 2 * i + k
            vs, es = residual(vv1[0], rr1[0], a, ops1)
            vc, ec = residual(vv1[1], rr1[1], a, ops1)
            rs = r1[0, a]
            num1 = num1 + fold((ec * vs + vc * rs)[own_y])
            den1 = den1 + fold((es * vs + vs * rs)[own_y])
            pair.append((es, ec))
        for v in range(2):
            t1[v, i * b1y : (i + 1) * b1y, :] = (pair[0][v] + pair[1][v])[own_y]
    t1y[...] = mm(t1[0], zc1) + mm(t1[1], zc1b)
    own2 = 0.125 * pair_rows(t1y, b2x * b2y)
    sr2[...] = own2
    gr[ino, iw] = own2
    num_row = jnp.sum(num0 + 8.0 * num1, axis=0, keepdims=True)
    den_row = jnp.sum(den0 + 8.0 * den1, axis=0, keepdims=True)
    row8 = iota((8, 128), 0)
    part = jnp.where(row8 == 0, num_row, jnp.where(row8 == 1, den_row, 0.0))
    sp2[...] = part
    gp[iw] = part
    over_wide(*gather_r, "start")
    over_wide(*gather_p, "start")

    over_narrow(*spread_m, "recv")

    def unpack(src, dst):
        def step(w, _):
            for n in range(nn):
                for i in range(b2x):
                    dst[PAD + w * b2x + i, n * b2y : (n + 1) * b2y, :] = src[n, w, i * b2y : (i + 1) * b2y, :]
            return 0

        lax.fori_loop(0, nw, step, 0)

    unpack(gm, v2)
    build(v2, cx2, cy2, cz2, rd2, None, PAD, PAD + x2, BASE_TAU / 16, z2, 4)

    def coarsen_pairs(get, xc, rows, dst):
        half = rows // 2

        def step(g, _):
            for k in range(4):
                a = PAD + 2 * (4 * g + k)
                t2[k * rows : (k + 1) * rows, :] = get(a) + get(a + 1)
            t2y[0 : 4 * rows, :] = mm(t2[0 : 4 * rows, :], zc1)
            flat = 0.125 * (t2y[pl.ds(0, 4 * half, stride=2), :] + t2y[pl.ds(1, 4 * half, stride=2), :])
            for k in range(4):
                dst[PAD + 4 * g + k, 0:half, :] = flat[k * half : (k + 1) * half]
            return 0

        lax.fori_loop(0, xc // 4, step, 0)

    v4[...] = jnp.zeros(v4.shape, F32)
    r4[...] = jnp.zeros(r4.shape, F32)
    coarsen_pairs(lambda a: v2[a], x3, v2.shape[1], v3)
    build(v3, cx3, cy3, cz3, rd3, None, PAD, PAD + x3, BASE_TAU / 64, z2 // 2, 4)
    coarsen_pairs(lambda a: v3[a], x4, v3.shape[1], v4)
    build(v4, cx4, cy4, cz4, rd4, None, PAD, PAD + x4, BASE_TAU / 256, z2 // 4, 4)

    over_wide(*gather_r, "recv")
    over_narrow(*spread_r, "start")
    over_wide(*gather_p, "recv")
    total = gp[0]
    if nw <= 16:
        for w in range(1, nw):
            total = total + gp[w]
    else:
        total = lax.fori_loop(1, nw, lambda w, acc: acc + gp[w], total)
    pb[...] = total
    over_narrow(*spread_p, "start")
    over_narrow(*spread_r, "recv")
    unpack(gr, r2)

    ops2 = (cx2, cy2, cz2, rd2, None)
    ops3 = (cx3, cy3, cz3, rd3, None)
    ops4 = (cx4, cy4, cz4, rd4, None)

    def down(u, v, r, ops, xc):
        def first(a):
            u[a] = ops[3][a] * r[a]

        slabs(PAD, PAD + xc, 4, first)
        sweep((u,), (v,), (r,), ops, PAD, PAD + xc, 4)

    def up(v, coarse, xc, rows):
        half = rows // 2

        def step(g, _):
            for k in range(4):
                t2[8 * k : 8 * k + 8, :] = coarse[PAD + 4 * g + k]
            wide_rows = mm(t2[0:32, :], zr)
            t2y[pl.ds(0, 32, stride=2), :] = wide_rows
            t2y[pl.ds(1, 32, stride=2), :] = wide_rows
            for k in range(4):
                add = t2y[16 * k : 16 * k + rows, :]
                a = PAD + 2 * (4 * g + k)
                v[a] = v[a] + add
                v[a + 1] = v[a + 1] + add
            return 0

        lax.fori_loop(0, xc // 4, step, 0)

    down(u2, v2, r2, ops2, x2)
    coarsen_pairs(lambda a: residual(v2, r2, a, ops2)[1], x3, v2.shape[1], r3)
    down(u3, v3, r3, ops3, x3)
    coarsen_pairs(lambda a: residual(v3, r3, a, ops3)[1], x4, v3.shape[1], r4)
    down(u4, v4, r4, ops4, x4)
    up(v3, v4, x4, v3.shape[1])
    sweep((v3,), (u3,), (r3,), ops3, PAD, PAD + x3, 4)
    sweep((u3,), (v3,), (r3,), ops3, PAD, PAD + x3, 4)
    up(v2, v3, x3, v2.shape[1])
    sweep((v2,), (u2,), (r2,), ops2, PAD, PAD + x2, 4)
    sweep((u2,), (v2,), (r2,), ops2, PAD, PAD + x2, 4)

    low = iota(v2.shape[1:], 1) < z2

    def dots(i, carry):
        num, den = carry
        for k in range(4):
            a = PAD + 4 * i + k
            both = jnp.where(low, v2[a], 0.0)
            den = den + fold(both * r2[a])
            num = num + fold(both * shift(r2[a], z2, 1))
        return num, den

    num2, den2 = lax.fori_loop(0, x2 // 4, dots, (zero8, zero8))
    over_narrow(*spread_p, "recv")
    whole = total
    for j in range(1, nn):
        whole = whole + pbs[lax.rem(ino + j, nn)]
    num = jnp.sum(jnp.where(row8 == 0, whole, 0.0) + 64.0 * num2)
    den = jnp.sum(jnp.where(row8 == 1, whole, 0.0) + 64.0 * den2)
    ratio = (jnp.full((8, 128), num) / (1.0 + jnp.full((8, 128), den)))[0:1, :]

    rows2 = v2.shape[1]
    full_y = 2 * rows2
    for i in range(b2x + 4):
        e = v2[PAD + iw * b2x - 2 + i]
        f1[i * rows2 : (i + 1) * rows2, :] = shift(e, z2, 1) - ratio * e
    fine = mm(f1[...], zr)
    for i in range(b2x + 4):
        part = fine[i * rows2 : (i + 1) * rows2]
        f1p[i, 0:b1y, :] = jnp.zeros((b1y, z1), F32)
        f1p[i, b1y + full_y : 2 * b1y + full_y, :] = jnp.zeros((b1y, z1), F32)
        f1p[i, pl.ds(b1y, rows2, stride=2), :] = part
        f1p[i, pl.ds(b1y + 1, rows2, stride=2), :] = part
    window = pl.ds(pl.multiple_of(ino * b1y, 8), 3 * b1y)
    for a in range(2, b1x + 2 * H1 - 2):
        i = (a - H1) // 2 + 2
        u1[0, a] = v1[1, a] - ratio * v1[0, a] + f1p[i, window, :]
        w1[a] = r1[1, a] - ratio * r1[0, a]
    sweep((u1.at[0],), (u1.at[1],), (w1,), ops1, 3, b1x + 2 * H1 - 3, 2)
    sweep((u1.at[1],), (u1.at[0],), (w1,), ops1, 4, b1x + 2 * H1 - 4, 2)

    rows1 = 3 * b1y
    zr0 = spread_matrix(z1, nz)
    ratio0 = jnp.concatenate([ratio] * (nz // 128), axis=1)
    for i in range(b1x + 2):
        part = mm(u1[0, H1 - 1 + i], zr0)
        for ref, lanes in ((f0a, slice(0, 128)), (f0b, slice(128, 256))):
            ref[i, pl.ds(0, rows1, stride=2), :] = part[:, lanes]
            ref[i, pl.ds(1, rows1, stride=2), :] = part[:, lanes]
    y_at = 2 * b1y - H0

    def up0(i, _):
        add = jnp.concatenate([f0a[i, y_at : y_at + m0.shape[1], :], f0b[i, y_at : y_at + m0.shape[1], :]], axis=1)
        for k in range(2):
            a = H0 - 2 + 2 * i + k
            us0[a] = vc0[a] - ratio0 * vs0[a] + add
            rc0[a] = rc0[a] - ratio0 * rs0[a]
        return 0

    lax.fori_loop(0, b1x + 2, up0, 0)
    sweep((us0,), (uc0,), (rc0,), ops0, 3, xs0 - 3, 1)

    def last(a):
        own, t = neighbours(uc0, a, cx0, cy0, cz0)
        out_ref[a - H0] = (KEEP * own + rd0[a] * (rc0[a] + t))[H0 : H0 + by]

    slabs(H0, H0 + bx, 1, last)

    each(lambda k: e0_copies(k, False), lambda c: c.wait_send())
    each(lambda k: e0_copies(k, False, 1), lambda c: c.wait_send(), (0, 1))
    each(lambda k: level1_copies(m1, m1s, m1r, k, False, 5), lambda c: c.wait_send())
    each(lambda k: level1_copies(r1, e1s, e1r, k, False, 4), lambda c: c.wait_send())
    over_wide(*gather_m, "send")
    over_wide(*gather_r, "send")
    over_wide(*gather_p, "send")
    over_narrow(*spread_m, "send")
    over_narrow(*spread_r, "send")
    over_narrow(*spread_p, "send")


def solution(mesh):
    nw, nn = mesh.shape["wide"], mesh.shape["narrow"]

    def per_device(mobility, sav_vector, cotangent):
        bx, by, nz = mobility.shape
        b1x, b1y, z1 = bx // 2, by // 2, nz // 2
        x2, y2 = nw * bx // 4, nn * by // 4
        vm = lambda *s: pltpu.VMEM(s, F32)
        dma = lambda *s: pltpu.SemaphoreType.DMA(s)
        l0 = (bx + 2 * H0, by + 2 * H0, nz)
        l1 = (b1x + 2 * H1, 3 * b1y, z1)
        l2 = (x2 + 2 * PAD, y2, z1)
        l3 = (x2 // 2 + 2 * PAD, y2 // 2, z1)
        l4 = (x2 // 4 + 2 * PAD, 8, z1)
        own2 = (bx // 4 * (by // 4), z1)
        scratch = (
            [vm(*l0)] * 12
            + [vm(2, 10, bx, nz), vm(2, 10, bx, nz), vm(2, 10, bx, nz), vm(4, 24, nz), vm(4, 24, nz)]
            + [vm(1, *l1)] + [vm(*l1)] * 5 + [vm(2, *l1)] * 3 + [vm(*l1)]
            + [vm(*l2)] * 7 + [vm(*l3)] * 7 + [vm(*l4)] * 7
            + [vm(2, b1x * by, nz), vm(b1x * by, z1), vm(2, bx // 4 * b1y, z1), vm(bx // 4 * b1y, z1)]
            + [vm(*own2), vm(*own2), vm(8, 128), vm(nn, nw, *own2), vm(nn, nw, *own2), vm(nw, 8, 128),
               vm(8, 128), vm(nn, 8, 128)]
            + [vm(64, z1), vm(64, z1)]
            + [vm((bx // 4 + 4) * y2, z1), vm(bx // 4 + 4, 2 * y2 + 2 * b1y, z1)]
            + [vm(b1x + 2, 6 * b1y, 128)] * 2
            + [dma(8, 6), dma(8, 6), dma(8, 1), dma(8, 1), dma(8, 2), dma(8, 2)]
            + [dma(nw), dma(nw), dma(nn), dma(nn)] + [dma(nw)] * 4 + [dma(nn)] * 4
        )
        return pl.pallas_call(
            functools.partial(kernel, nw, nn, bx, by, nz),
            out_shape=jax.ShapeDtypeStruct((bx, by, nz), F32),
            in_specs=[pl.BlockSpec(memory_space=pltpu.VMEM)] * 3,
            out_specs=pl.BlockSpec(memory_space=pltpu.VMEM),
            scratch_shapes=scratch,
            compiler_params=pltpu.CompilerParams(
                collective_id=0, has_side_effects=True, vmem_limit_bytes=67043328
            ),
        )(mobility, sav_vector, cotangent)

    spec = P("wide", "narrow", None)
    return jax.shard_map(per_device, mesh=mesh, in_specs=(spec,) * 3, out_specs=spec, check_vma=False)
```

```python
import functools
import jax
import jax.numpy as jnp
from jax import lax
from jax.experimental import pallas as pl
from jax.experimental.pallas import tpu as pltpu
from jax.sharding import PartitionSpec as P

DAMPING = 0.8
KEEP = 1.0 - DAMPING
BASE_TAU = 16.0
H0 = 4
H1 = 5
PAD = 2
MESH = pl.DeviceIdType.MESH
F32 = jnp.float32
SIDES = [(-1, 0), (1, 0), (0, -1), (0, 1), (-1, -1), (-1, 1), (1, -1), (1, 1)]
OPPOSITE = [1, 0, 3, 2, 7, 6, 5, 4]


def iota(shape, dim):
    return lax.broadcasted_iota(jnp.int32, shape, dim)


def shift(value, amount, axis):
    return pltpu.roll(value, amount % value.shape[axis], axis)


def squeeze_matrix(rows, cols, offset=0):
    i, j = iota((rows, cols), 0), iota((rows, cols), 1)
    k = i - 2 * (j - offset)
    return jnp.where((k == 0) | (k == 1), 1.0, 0.0).astype(F32)


def spread_matrix(rows, cols):
    i, j = iota((rows, cols), 0), iota((rows, cols), 1)
    k = j - 2 * i
    return jnp.where((k == 0) | (k == 1), 1.0, 0.0).astype(F32)


def mm(a, b):
    return jnp.dot(a, b, precision=lax.Precision.HIGHEST, preferred_element_type=F32)


def rounded(x):
    return x.astype(jnp.bfloat16).astype(F32)


def slabs(lo, hi, chunk, body):
    def step(i, _):
        for k in range(chunk):
            body(lo + i * chunk + k)
        return 0

    lax.fori_loop(0, (hi - lo) // chunk, step, 0)


def build(m, cx, cy, cz, rd, d, lo, hi, tau, seg, chunk):
    shape = m.shape[1:]
    row = iota(shape, 0)
    lane = lax.rem(iota(shape, 1), seg)
    last_row, first_row = row == shape[0] - 1, row == 0
    last_lane, first_lane = lane == seg - 1, lane == 0
    half = 0.5 * tau

    def body(a):
        own = m[a]
        xp, xm = m[a + 1], m[a - 1]
        yp = jnp.where(last_row, 0.0, shift(own, -1, 0))
        ym = jnp.where(first_row, 0.0, shift(own, 1, 0))
        zp = jnp.where(last_lane, 0.0, shift(own, -1, 1))
        zm = jnp.where(first_lane, 0.0, shift(own, 1, 1))
        total = 1.0
        for other, ref in ((xp, cx), (xm, None), (yp, cy), (ym, None), (zp, cz), (zm, None)):
            face = rounded(half * (own + other))
            total = total + face
            if ref is not None:
                ref[a] = jnp.where(jnp.minimum(own, other) > 0.0, face, 0.0)
        rd[a] = DAMPING / total
        if d is not None:
            d[a] = total

    slabs(lo, hi, chunk, body)


def pairs(lo, hi):
    return 2 - (hi - lo) % 2


def neighbours(v, a, cx, cy, cz):
    own = v[a]
    cya, cza = cy[a], cz[a]
    total = cx[a] * v[a + 1] + cx[a - 1] * v[a - 1]
    total = total + (cya * shift(own, -1, 0) + shift(cya * own, 1, 0))
    total = total + (cza * shift(own, -1, 1) + shift(cza * own, 1, 1))
    return own, total


def sweep(vin, vout, r, ops, lo, hi, chunk):
    cx, cy, cz, rd, d = ops

    def body(a):
        for vi, vo, ri in zip(vin, vout, r):
            own, t = neighbours(vi, a, cx, cy, cz)
            vo[a] = KEEP * own + rd[a] * (ri[a] + t)

    slabs(lo, hi, chunk, body)


def residual(vi, ri, a, ops):
    cx, cy, cz, rd, d = ops
    own, t = neighbours(vi, a, cx, cy, cz)
    diag = d[a] if d is not None else DAMPING / rd[a]
    return own, ri[a] + t - diag * own


def fold(x):
    total = None
    for i in range(x.shape[0] // 8):
        for j in range(x.shape[1] // 128):
            part = x[8 * i : 8 * i + 8, 128 * j : 128 * j + 128]
            total = part if total is None else total + part
    return total


def kernel(nw, nn, bx, by, nz, m_ref, s_ref, c_ref, out_ref,
           m0, cx0, cy0, cz0, rd0, d0, rs0, rc0, us0, uc0, vs0, vc0,
           rx, yp, ry, cp, rcn,
           m1, cx1, cy1, cz1, rd1, d1, r1, u1, v1, w1,
           cx2, cy2, cz2, rd2, r2, u2, v2,
           cx3, cy3, cz3, rd3, r3, u3, v3,
           cx4, cy4, cz4, rd4, r4, u4, v4,
           t0, t0y, t1, t1y, sm2, sr2, sp2, gm, gr, gp, pb, pbs, t2, t2y, f1, f1p, f0a, f0b,
           e0s, e0r, m1s, m1r, e1s, e1r,
           ams, amr, bms, bmr, ars, arr, aps, apr, brs, brr, bps, bpr):
    iw, ino = lax.axis_index("wide"), lax.axis_index("narrow")
    b1x, b1y, z1 = bx // 2, by // 2, nz // 2
    b2x, b2y, z2 = bx // 4, by // 4, nz // 4
    x2, x3, x4 = nw * b2x, nw * b2x // 2, nw * b2x // 4
    xs0 = bx + 2 * H0
    there = []
    for dx, dy in SIDES:
        ok = None
        for cond, on in ((iw > 0, dx < 0), (iw < nw - 1, dx > 0), (ino > 0, dy < 0), (ino < nn - 1, dy > 0)):
            if on:
                ok = cond if ok is None else jnp.logical_and(ok, cond)
        there.append(ok)

    def peer(side):
        return (iw + SIDES[side][0], ino + SIDES[side][1])

    barrier = pltpu.get_barrier_semaphore()

    def greet(j, _):
        pl.semaphore_signal(barrier, inc=1, device_id=(lax.rem(iw + j, nw), ino), device_id_type=MESH)
        return 0

    lax.fori_loop(1, nw, greet, 0)
    for j in range(1, nn):
        pl.semaphore_signal(barrier, inc=1, device_id=(iw, lax.rem(ino + j, nn)), device_id_type=MESH)
    for k in range(4, 8):
        @pl.when(there[k])
        def _():
            pl.semaphore_signal(barrier, inc=1, device_id=peer(k), device_id_type=MESH)

    for side, (m_lo, r_lo) in enumerate(((0, 0), (by - 4, by - 3))):
        for k in range(4):
            yp[side, k] = m_ref[:, m_lo + k, :]
        for k in range(3):
            yp[side, 4 + k] = s_ref[:, r_lo + k, :]
            yp[side, 7 + k] = c_ref[:, r_lo + k, :]
    for k in range(4, 8):
        dx, dy = SIDES[k]
        m_x, m_y = (0 if dx < 0 else bx - 3), (0 if dy < 0 else by - 3)
        r_x, r_y = (0 if dx < 0 else bx - 2), (0 if dy < 0 else by - 2)
        for i in range(3):
            cp[k - 4, 3 * i : 3 * i + 3, :] = m_ref[m_x + i, m_y : m_y + 3, :]
        for i in range(2):
            cp[k - 4, 9 + 2 * i : 11 + 2 * i, :] = s_ref[r_x + i, r_y : r_y + 2, :]
            cp[k - 4, 13 + 2 * i : 15 + 2 * i, :] = c_ref[r_x + i, r_y : r_y + 2, :]

    beside_x = jnp.minimum(iw, 1) + jnp.minimum(nw - 1 - iw, 1)
    beside_y = jnp.minimum(ino, 1) + jnp.minimum(nn - 1 - ino, 1)
    pl.semaphore_wait(barrier, nw + nn - 2 + beside_x * beside_y)

    def remote(src, dst, ssem, rsem, dev):
        return pltpu.make_async_remote_copy(src_ref=src, dst_ref=dst, send_sem=ssem, recv_sem=rsem,
                                            device_id=dev, device_id_type=MESH)

    def e0_copies(side, recv, wave=0):
        other = OPPOSITE[side]
        land = side if recv else other
        dev = peer(side)
        if side < 2:
            out = []
            at = 0
            for n, (ref, width) in enumerate(((m_ref, 4), (s_ref, 3), (c_ref, 3))):
                lo = 0 if side == 0 else bx - width
                skip = width - 1 if side == 0 else 0
                first = 0 if side == 0 else 1
                if wave == 1:
                    out.append(remote(ref.at[lo + skip : lo + skip + 1], rx.at[land, at + skip : at + skip + 1],
                                      e0s.at[side, 3 + n], e0r.at[land, 3 + n], dev))
                else:
                    out.append(remote(ref.at[lo + first : lo + first + width - 1],
                                      rx.at[land, at + first : at + first + width - 1],
                                      e0s.at[side, n], e0r.at[land, n], dev))
                at += width
            return out
        if side < 4:
            return [remote(yp.at[side - 2], ry.at[land - 2], e0s.at[side, 0], e0r.at[land, 0], dev)]
        return [remote(cp.at[side - 4], rcn.at[land - 4], e0s.at[side, 0], e0r.at[land, 0], dev)]

    def box1(side, sending, width):
        dx, dy = SIDES[side]
        own = H1
        if sending:
            xlo, w = (own, width) if dx < 0 else ((own + b1x - width, width) if dx > 0 else (own, b1x))
            ylo = b1y
        else:
            xlo, w = (own - width, width) if dx < 0 else ((own + b1x, width) if dx > 0 else (own, b1x))
            ylo = b1y * (1 + dy)
        return xlo, w, ylo

    def level1_copies(ref, ssem, rsem, side, recv, width):
        land = side if recv else OPPOSITE[side]
        sx, w, sy = box1(side, True, width)
        tx, _, ty = box1(land, False, width)
        return [remote(ref.at[v, sx : sx + w, sy : sy + b1y], ref.at[v, tx : tx + w, ty : ty + b1y],
                       ssem.at[side, v], rsem.at[land, v], peer(side)) for v in range(ref.shape[0])]

    def each(fn, act, sides=range(8)):
        for side in sides:
            @pl.when(there[side])
            def _():
                for copy in fn(side):
                    act(copy)

    def start(copy):
        copy.start()

    each(lambda k: e0_copies(k, False), start, (0, 1, 4, 5, 6, 7, 2, 3))

    zc0 = squeeze_matrix(nz, z1)
    zc1 = squeeze_matrix(z1, z1)
    zc1b = squeeze_matrix(z1, z1, z2)
    zr = spread_matrix(z1, z1)

    def pair_rows(flat, half_rows):
        return flat[pl.ds(0, half_rows, stride=2), :] + flat[pl.ds(1, half_rows, stride=2), :]

    for i in range(b1x):
        t0[0, i * by : (i + 1) * by, :] = m_ref[2 * i] + m_ref[2 * i + 1]
    t0y[...] = mm(t0[0], zc0)
    mob1 = 0.125 * pair_rows(t0y, b1x * b1y)
    for i in range(b1x):
        m1[0, H1 + i, b1y : 2 * b1y, :] = mob1[i * b1y : (i + 1) * b1y]

    def clear1(ref, width):
        for side in range(8):
            xlo, w, ylo = box1(side, False, width)
            @pl.when(jnp.logical_not(there[side]))
            def _():
                ref[:, xlo : xlo + w, ylo : ylo + b1y, :] = jnp.zeros((ref.shape[0], w, b1y, z1), F32)

    clear1(m1, 5)
    clear1(r1, 4)
    each(lambda k: level1_copies(m1, m1s, m1r, k, False, 5), start)
    for i in range(b2x):
        t1[0, i * b1y : (i + 1) * b1y, :] = mob1[2 * i * b1y : (2 * i + 1) * b1y] + mob1[(2 * i + 1) * b1y : (2 * i + 2) * b1y]
    t1y[...] = mm(t1[0], zc1 + zc1b)
    mob2 = 0.125 * pair_rows(t1y, b2x * b2y)
    sm2[...] = mob2
    gm[ino, iw] = mob2

    def wide_copy(src, dst_ref, ssem, rsem, j, recv):
        to = lax.rem(iw + j, nw)
        if recv:
            return remote(src, dst_ref(to), ssem.at[j], rsem.at[to], (to, ino))
        return remote(src, dst_ref(iw), ssem.at[j], rsem.at[iw], (to, ino))

    def over_wide(src, dst_ref, ssem, rsem, what):
        def step(j, _):
            copy = wide_copy(src, dst_ref, ssem, rsem, j, what == "recv")
            if what == "start":
                copy.start()
            elif what == "recv":
                copy.wait_recv()
            else:
                copy.wait_send()
            return 0

        lax.fori_loop(1, nw, step, 0)

    def over_narrow(src, dst_ref, ssem, rsem, what):
        for j in range(1, nn):
            to = lax.rem(ino + j, nn)
            if what == "recv":
                remote(src, dst_ref(to), ssem.at[j], rsem.at[to], (iw, to)).wait_recv()
            else:
                copy = remote(src, dst_ref(ino), ssem.at[j], rsem.at[ino], (iw, to))
                if what == "start":
                    copy.start()
                else:
                    copy.wait_send()

    gather_m = (sm2, lambda w: gm.at[ino, w], ams, amr)
    spread_m = (gm.at[ino], lambda n: gm.at[n], bms, bmr)
    gather_r = (sr2, lambda w: gr.at[ino, w], ars, arr)
    gather_p = (sp2, lambda w: gp.at[w], aps, apr)
    spread_r = (gr.at[ino], lambda n: gr.at[n], brs, brr)
    spread_p = (pb, lambda n: pbs.at[n], bps, bpr)
    each(lambda k: e0_copies(k, False, 1), start, (0, 1))
    over_wide(*gather_m, "start")

    blank = jnp.zeros((H0, m0.shape[1], nz), F32)
    for ref, src in ((m0, m_ref), (rs0, s_ref), (rc0, c_ref)):
        ref[0:H0] = blank
        ref[H0 + bx :] = blank

        def put(i, _):
            ref[H0 + i, H0 : H0 + by, :] = src[i]
            return 0

        lax.fori_loop(0, bx, put, 0)
    for ref in (u2, v2, u3, v3, u4, v4):
        zero = jnp.zeros(ref.shape[1:], F32)
        for a in (0, 1, ref.shape[0] - 2, ref.shape[0] - 1):
            ref[a] = zero
    for ref in (cx2, cx3, cx4):
        ref[PAD - 1] = jnp.zeros(ref.shape[1:], F32)
    for k in range(2):
        @pl.when(jnp.logical_not(there[k]))
        def _():
            rx[k] = jnp.zeros(rx.shape[1:], F32)

        @pl.when(jnp.logical_not(there[2 + k]))
        def _():
            ry[k] = jnp.zeros(ry.shape[1:], F32)
    for k in range(4):
        @pl.when(jnp.logical_not(there[4 + k]))
        def _():
            rcn[k] = jnp.zeros(rcn.shape[1:], F32)

    def landed(copy):
        copy.wait_recv()

    each(lambda k: e0_copies(k, True), landed, (2, 3))
    fields = ((m0, 0, 4), (rs0, 4, 3), (rc0, 7, 3))
    for ref, at, width in fields:
        for i in range(width):
            ref[H0 : H0 + bx, H0 - width + i, :] = ry[0, at + i]
            ref[H0 : H0 + bx, H0 + by + i, :] = ry[1, at + i]

    ops0 = (cx0, cy0, cz0, rd0, d0)

    def first0(a):
        us0[a] = rd0[a] * rs0[a]
        uc0[a] = rd0[a] * rc0[a]

    def start0(lo, hi, v_lo, v_hi):
        build(m0, cx0, cy0, cz0, rd0, d0, lo, hi, BASE_TAU, nz, pairs(lo, hi))
        slabs(lo, hi, 1, first0)
        if v_hi > v_lo:
            sweep((us0, uc0), (vs0, vc0), (rs0, rc0), ops0, v_lo, v_hi, pairs(v_lo, v_hi))

    start0(H0 + 1, H0 + bx - 1, H0 + 2, H0 + bx - 2)

    def down0(i, carry):
        num, den = carry
        sums = []
        for k in range(2):
            a = H0 + 2 * i + k
            vs, es = residual(vs0, rs0, a, ops0)
            vc, ec = residual(vc0, rc0, a, ops0)
            rs = rs0[a]
            num = num + fold((ec * vs + vc * rs)[H0 : H0 + by])
            den = den + fold((es * vs + vs * rs)[H0 : H0 + by])
            sums.append((es, ec))
        at = pl.ds(pl.multiple_of(i * by, by), by)
        t0[0, at, :] = (sums[0][0] + sums[1][0])[H0 : H0 + by]
        t0[1, at, :] = (sums[0][1] + sums[1][1])[H0 : H0 + by]
        return num, den

    zero8 = jnp.zeros((8, 128), F32)
    part0 = lax.fori_loop(2, b1x - 2, down0, (zero8, zero8))

    each(lambda k: e0_copies(k, True), landed, (0, 1, 4, 5, 6, 7))
    for ref, at, width in fields:
        for i in range(width - 1):
            ref[H0 - width + 1 + i, H0 : H0 + by, :] = rx[0, at + 1 + i]
            ref[H0 + bx + i, H0 : H0 + by, :] = rx[1, at + i]
    for k in range(4):
        dx, dy = SIDES[4 + k]
        m_x, m_y = (H0 - 3 if dx < 0 else H0 + bx), (H0 - 3 if dy < 0 else H0 + by)
        r_x, r_y = (H0 - 2 if dx < 0 else H0 + bx), (H0 - 2 if dy < 0 else H0 + by)
        for i in range(3):
            m0[m_x + i, m_y : m_y + 3, :] = rcn[k, 3 * i : 3 * i + 3, :]
        for i in range(2):
            rs0[r_x + i, r_y : r_y + 2, :] = rcn[k, 9 + 2 * i : 11 + 2 * i, :]
            rc0[r_x + i, r_y : r_y + 2, :] = rcn[k, 13 + 2 * i : 15 + 2 * i, :]
    for lo, hi, v_lo, v_hi in ((2, H0 + 1, 3, H0 + 2), (H0 + bx - 1, xs0 - 2, H0 + bx - 2, xs0 - 3)):
        build(m0, cx0, cy0, cz0, rd0, d0, lo, hi, BASE_TAU, nz, pairs(lo, hi))
        slabs(lo, hi, 1, first0)
        sweep((us0, uc0), (vs0, vc0), (rs0, rc0), ops0, v_lo, v_hi, pairs(v_lo, v_hi))
    part0 = lax.fori_loop(0, 2, down0, part0)
    num0, den0 = lax.fori_loop(b1x - 2, b1x, down0, part0)
    for v in range(2):
        t0y[...] = mm(t0[v], zc0)
        coarse = 0.125 * pair_rows(t0y, b1x * b1y)
        for i in range(b1x):
            r1[v, H1 + i, b1y : 2 * b1y, :] = coarse[i * b1y : (i + 1) * b1y]
    each(lambda k: level1_copies(r1, e1s, e1r, k, False, 4), start)

    each(lambda k: e0_copies(k, True, 1), landed, (0, 1))
    for ref, at, width in fields:
        ref[H0 - width, H0 : H0 + by, :] = rx[0, at]
        ref[H0 + bx + width - 1, H0 : H0 + by, :] = rx[1, at + width - 1]
    for lo, v_lo in ((1, 2), (xs0 - 2, xs0 - 3)):
        start0(lo, lo + 1, v_lo, v_lo + 1)
    each(lambda k: level1_copies(m1, m1s, m1r, k, True, 5), lambda c: c.wait_recv())
    ops1 = (cx1, cy1, cz1, rd1, d1)
    build(m1.at[0], cx1, cy1, cz1, rd1, d1, 1, b1x + 2 * H1 - 1, BASE_TAU / 4, z1, 2)
    over_wide(*gather_m, "recv")
    over_narrow(*spread_m, "start")

    each(lambda k: level1_copies(r1, e1s, e1r, k, True, 4), lambda c: c.wait_recv())
    rr1 = (r1.at[0], r1.at[1])
    uu1 = (u1.at[0], u1.at[1])
    vv1 = (v1.at[0], v1.at[1])

    def first1(a):
        for v in range(2):
            u1[v, a] = rd1[a] * r1[v, a]

    slabs(1, b1x + 2 * H1 - 1, 2, first1)
    sweep(uu1, vv1, rr1, ops1, 2, b1x + 2 * H1 - 2, 2)
    num1, den1 = zero8, zero8
    own_y = slice(b1y, 2 * b1y)
    for i in range(b2x):
        pair = []
        for k in range(2):
            a = H1 + 2 * i + k
            vs, es = residual(vv1[0], rr1[0], a, ops1)
            vc, ec = residual(vv1[1], rr1[1], a, ops1)
            rs = r1[0, a]
            num1 = num1 + fold((ec * vs + vc * rs)[own_y])
            den1 = den1 + fold((es * vs + vs * rs)[own_y])
            pair.append((es, ec))
        for v in range(2):
            t1[v, i * b1y : (i + 1) * b1y, :] = (pair[0][v] + pair[1][v])[own_y]
    t1y[...] = mm(t1[0], zc1) + mm(t1[1], zc1b)
    own2 = 0.125 * pair_rows(t1y, b2x * b2y)
    sr2[...] = own2
    gr[ino, iw] = own2
    num_row = jnp.sum(num0 + 8.0 * num1, axis=0, keepdims=True)
    den_row = jnp.sum(den0 + 8.0 * den1, axis=0, keepdims=True)
    row8 = iota((8, 128), 0)
    part = jnp.where(row8 == 0, num_row, jnp.where(row8 == 1, den_row, 0.0))
    sp2[...] = part
    gp[iw] = part
    over_wide(*gather_r, "start")
    over_wide(*gather_p, "start")

    over_narrow(*spread_m, "recv")

    def unpack(src, dst):
        def step(w, _):
            for n in range(nn):
                for i in range(b2x):
                    dst[PAD + w * b2x + i, n * b2y : (n + 1) * b2y, :] = src[n, w, i * b2y : (i + 1) * b2y, :]
            return 0

        lax.fori_loop(0, nw, step, 0)

    unpack(gm, v2)
    build(v2, cx2, cy2, cz2, rd2, None, PAD, PAD + x2, BASE_TAU / 16, z2, 8)

    def coarsen_pairs(get, xc, rows, dst):
        half = rows // 2

        def step(g, _):
            for k in range(4):
                a = PAD + 2 * (4 * g + k)
                t2[k * rows : (k + 1) * rows, :] = get(a) + get(a + 1)
            t2y[0 : 4 * rows, :] = mm(t2[0 : 4 * rows, :], zc1)
            flat = 0.125 * (t2y[pl.ds(0, 4 * half, stride=2), :] + t2y[pl.ds(1, 4 * half, stride=2), :])
            for k in range(4):
                dst[PAD + 4 * g + k, 0:half, :] = flat[k * half : (k + 1) * half]
            return 0

        lax.fori_loop(0, xc // 4, step, 0)

    v4[...] = jnp.zeros(v4.shape, F32)
    r4[...] = jnp.zeros(r4.shape, F32)
    coarsen_pairs(lambda a: v2[a], x3, v2.shape[1], v3)
    build(v3, cx3, cy3, cz3, rd3, None, PAD, PAD + x3, BASE_TAU / 64, z2 // 2, 4)
    coarsen_pairs(lambda a: v3[a], x4, v3.shape[1], v4)
    build(v4, cx4, cy4, cz4, rd4, None, PAD, PAD + x4, BASE_TAU / 256, z2 // 4, 4)

    over_wide(*gather_r, "recv")
    over_narrow(*spread_r, "start")
    over_wide(*gather_p, "recv")
    total = gp[0]
    if nw <= 16:
        for w in range(1, nw):
            total = total + gp[w]
    else:
        total = lax.fori_loop(1, nw, lambda w, acc: acc + gp[w], total)
    pb[...] = total
    over_narrow(*spread_p, "start")
    over_narrow(*spread_r, "recv")
    unpack(gr, r2)

    ops2 = (cx2, cy2, cz2, rd2, None)
    ops3 = (cx3, cy3, cz3, rd3, None)
    ops4 = (cx4, cy4, cz4, rd4, None)

    def down(u, v, r, ops, xc):
        def first(a):
            u[a] = ops[3][a] * r[a]

        slabs(PAD, PAD + xc, 4, first)
        sweep((u,), (v,), (r,), ops, PAD, PAD + xc, 8)

    def up(v, coarse, xc, rows):
        half = rows // 2

        def step(g, _):
            for k in range(4):
                t2[8 * k : 8 * k + 8, :] = coarse[PAD + 4 * g + k]
            wide_rows = mm(t2[0:32, :], zr)
            t2y[pl.ds(0, 32, stride=2), :] = wide_rows
            t2y[pl.ds(1, 32, stride=2), :] = wide_rows
            for k in range(4):
                add = t2y[16 * k : 16 * k + rows, :]
                a = PAD + 2 * (4 * g + k)
                v[a] = v[a] + add
                v[a + 1] = v[a + 1] + add
            return 0

        lax.fori_loop(0, xc // 4, step, 0)

    down(u2, v2, r2, ops2, x2)
    coarsen_pairs(lambda a: residual(v2, r2, a, ops2)[1], x3, v2.shape[1], r3)
    down(u3, v3, r3, ops3, x3)
    coarsen_pairs(lambda a: residual(v3, r3, a, ops3)[1], x4, v3.shape[1], r4)
    down(u4, v4, r4, ops4, x4)
    up(v3, v4, x4, v3.shape[1])
    sweep((v3,), (u3,), (r3,), ops3, PAD, PAD + x3, 8)
    sweep((u3,), (v3,), (r3,), ops3, PAD, PAD + x3, 8)
    up(v2, v3, x3, v2.shape[1])
    sweep((v2,), (u2,), (r2,), ops2, PAD, PAD + x2, 8)
    sweep((u2,), (v2,), (r2,), ops2, PAD, PAD + x2, 8)

    low = iota(v2.shape[1:], 1) < z2

    def dots(i, carry):
        num, den = carry
        for k in range(4):
            a = PAD + 4 * i + k
            both = jnp.where(low, v2[a], 0.0)
            den = den + fold(both * r2[a])
            num = num + fold(both * shift(r2[a], z2, 1))
        return num, den

    num2, den2 = lax.fori_loop(0, x2 // 4, dots, (zero8, zero8))
    over_narrow(*spread_p, "recv")
    whole = total
    for j in range(1, nn):
        whole = whole + pbs[lax.rem(ino + j, nn)]
    num = jnp.sum(jnp.where(row8 == 0, whole, 0.0) + 64.0 * num2)
    den = jnp.sum(jnp.where(row8 == 1, whole, 0.0) + 64.0 * den2)
    ratio = (jnp.full((8, 128), num) / (1.0 + jnp.full((8, 128), den)))[0:1, :]

    rows2 = v2.shape[1]
    full_y = 2 * rows2
    for i in range(b2x + 4):
        e = v2[PAD + iw * b2x - 2 + i]
        f1[i * rows2 : (i + 1) * rows2, :] = shift(e, z2, 1) - ratio * e
    fine = mm(f1[...], zr)
    for i in range(b2x + 4):
        part = fine[i * rows2 : (i + 1) * rows2]
        f1p[i, 0:b1y, :] = jnp.zeros((b1y, z1), F32)
        f1p[i, b1y + full_y : 2 * b1y + full_y, :] = jnp.zeros((b1y, z1), F32)
        f1p[i, pl.ds(b1y, rows2, stride=2), :] = part
        f1p[i, pl.ds(b1y + 1, rows2, stride=2), :] = part
    window = pl.ds(pl.multiple_of(ino * b1y, 8), 3 * b1y)
    for a in range(2, b1x + 2 * H1 - 2):
        i = (a - H1) // 2 + 2
        u1[0, a] = v1[1, a] - ratio * v1[0, a] + f1p[i, window, :]
        w1[a] = r1[1, a] - ratio * r1[0, a]
    sweep((u1.at[0],), (u1.at[1],), (w1,), ops1, 3, b1x + 2 * H1 - 3, 2)
    sweep((u1.at[1],), (u1.at[0],), (w1,), ops1, 4, b1x + 2 * H1 - 4, 2)

    rows1 = 3 * b1y
    zr0 = spread_matrix(z1, nz)
    ratio0 = jnp.concatenate([ratio] * (nz // 128), axis=1)
    for i in range(b1x + 2):
        part = mm(u1[0, H1 - 1 + i], zr0)
        for ref, lanes in ((f0a, slice(0, 128)), (f0b, slice(128, 256))):
            ref[i, pl.ds(0, rows1, stride=2), :] = part[:, lanes]
            ref[i, pl.ds(1, rows1, stride=2), :] = part[:, lanes]
    y_at = 2 * b1y - H0

    def up0(i, _):
        add = jnp.concatenate([f0a[i, y_at : y_at + m0.shape[1], :], f0b[i, y_at : y_at + m0.shape[1], :]], axis=1)
        for k in range(2):
            a = H0 - 2 + 2 * i + k
            us0[a] = vc0[a] - ratio0 * vs0[a] + add
            rc0[a] = rc0[a] - ratio0 * rs0[a]
        return 0

    lax.fori_loop(0, b1x + 2, up0, 0)
    sweep((us0,), (uc0,), (rc0,), ops0, 3, xs0 - 3, 2)

    def last(a):
        own, t = neighbours(uc0, a, cx0, cy0, cz0)
        out_ref[a - H0] = (KEEP * own + rd0[a] * (rc0[a] + t))[H0 : H0 + by]

    slabs(H0, H0 + bx, 2, last)

    each(lambda k: e0_copies(k, False), lambda c: c.wait_send())
    each(lambda k: e0_copies(k, False, 1), lambda c: c.wait_send(), (0, 1))
    each(lambda k: level1_copies(m1, m1s, m1r, k, False, 5), lambda c: c.wait_send())
    each(lambda k: level1_copies(r1, e1s, e1r, k, False, 4), lambda c: c.wait_send())
    over_wide(*gather_m, "send")
    over_wide(*gather_r, "send")
    over_wide(*gather_p, "send")
    over_narrow(*spread_m, "send")
    over_narrow(*spread_r, "send")
    over_narrow(*spread_p, "send")


def solution(mesh):
    nw, nn = mesh.shape["wide"], mesh.shape["narrow"]

    def per_device(mobility, sav_vector, cotangent):
        bx, by, nz = mobility.shape
        b1x, b1y, z1 = bx // 2, by // 2, nz // 2
        x2, y2 = nw * bx // 4, nn * by // 4
        vm = lambda *s: pltpu.VMEM(s, F32)
        dma = lambda *s: pltpu.SemaphoreType.DMA(s)
        l0 = (bx + 2 * H0, by + 2 * H0, nz)
        l1 = (b1x + 2 * H1, 3 * b1y, z1)
        l2 = (x2 + 2 * PAD, y2, z1)
        l3 = (x2 // 2 + 2 * PAD, y2 // 2, z1)
        l4 = (x2 // 4 + 2 * PAD, 8, z1)
        own2 = (bx // 4 * (by // 4), z1)
        scratch = (
            [vm(*l0)] * 12
            + [vm(2, 10, bx, nz), vm(2, 10, bx, nz), vm(2, 10, bx, nz), vm(4, 24, nz), vm(4, 24, nz)]
            + [vm(1, *l1)] + [vm(*l1)] * 5 + [vm(2, *l1)] * 3 + [vm(*l1)]
            + [vm(*l2)] * 7 + [vm(*l3)] * 7 + [vm(*l4)] * 7
            + [vm(2, b1x * by, nz), vm(b1x * by, z1), vm(2, bx // 4 * b1y, z1), vm(bx // 4 * b1y, z1)]
            + [vm(*own2), vm(*own2), vm(8, 128), vm(nn, nw, *own2), vm(nn, nw, *own2), vm(nw, 8, 128),
               vm(8, 128), vm(nn, 8, 128)]
            + [vm(64, z1), vm(64, z1)]
            + [vm((bx // 4 + 4) * y2, z1), vm(bx // 4 + 4, 2 * y2 + 2 * b1y, z1)]
            + [vm(b1x + 2, 6 * b1y, 128)] * 2
            + [dma(8, 6), dma(8, 6), dma(8, 1), dma(8, 1), dma(8, 2), dma(8, 2)]
            + [dma(nw), dma(nw), dma(nn), dma(nn)] + [dma(nw)] * 4 + [dma(nn)] * 4
        )
        return pl.pallas_call(
            functools.partial(kernel, nw, nn, bx, by, nz),
            out_shape=jax.ShapeDtypeStruct((bx, by, nz), F32),
            in_specs=[pl.BlockSpec(memory_space=pltpu.VMEM)] * 3,
            out_specs=pl.BlockSpec(memory_space=pltpu.VMEM),
            scratch_shapes=scratch,
            compiler_params=pltpu.CompilerParams(
                collective_id=0, has_side_effects=True, vmem_limit_bytes=67043328
            ),
        )(mobility, sav_vector, cotangent)

    spec = P("wide", "narrow", None)
    return jax.shard_map(per_device, mesh=mesh, in_specs=(spec,) * 3, out_specs=spec, check_vma=False)
```
